512 devices in a mesh: dp: 8 (over y, core), expert: 64 (over x, z).
Axes of the slice: x: 4, y: 4, z: 16, core: 2. Of those that a mesh axis runs over, the one named last changes fastest.
Arguments:
- tokens: bfloat16 [8192, 1024], P('expert'), may hold values from -6 to 6
- routes: int32 [8192, 6], P('expert'), may hold values from 0 to 63, all different within a row; in each aligned block of 128 rows (0 to 127, 128 to 255, ...) at most 16 rows name the same one
- route_gates: bfloat16 [8192, 6], P('expert'), may hold values from 0.049804688 to 0.5
- domains: int32 [8192], P('expert'), may hold values from 0 to 63
- domain_weight: float32 [64], replicated, may hold values from 0.25 to 4
- targets: bfloat16 [8192, 1024], P('expert'), may hold values from -6 to 6
- w_gate: bfloat16 [64, 1024, 1024], P('expert', None, 'dp'), may hold values from -0.1875 to 0.1875
- w_up: bfloat16 [64, 1024, 1024], P('expert', None, 'dp'), may hold values from -0.1875 to 0.1875
- w_down: bfloat16 [64, 1024, 1024], P('expert', 'dp'), may hold values from -0.1875 to 0.1875
Outputs:
- grad_tokens: bfloat16 [8192, 1024], P('expert')
- grad_gate: float32 [64, 1024, 1024], P('expert', None, 'dp')
- grad_up: float32 [64, 1024, 1024], P('expert', None, 'dp')
- grad_down: float32 [64, 1024, 1024], P('expert', 'dp')
The draws below stay inside these ranges and needn't reach their ends.
Inputs may be any that keep to these rules, and one draw needn't show every extreme that they name: `routes`: each row names 6 different experts. Among the rows of one block of 128 tokens no expert is named more than 16 times, and in every draw some block names some expert exactly 16 times.
All inputs are finite; a program needn't handle non-finite values.
Results may differ from the reference program's by a relative error of at most 0.015.
Values may be sent and summed in bfloat16 or wider, within the bound.
No kernel may reach another device: no remote copies, remote signals or barrier semaphores. Data moves between devices by JAX's collectives and lax.ppermute only.
A program may use at most 64 MiB of HBM per device.

```python
import math
import jax
import jax.numpy as jnp
import numpy as np
from jax import lax

D = 1024
FF = 1024
TOPK = 6
NDOM = 64
TOK_DEV = 128
EXPERTS = 64
CAP = 16
FF_DEV = 128
SLOTS = 1024
TOKENS = 8192
N_DP = 8


def with_ends(array, own_key, low, largest):
    longest = array.shape.index(max(array.shape))
    spots = []
    for shift in (0, 1):
        where = [jax.random.randint(jax.random.fold_in(own_key, axis), (), 0, length) for axis, length in enumerate(array.shape)]
        where[longest] = (where[longest] + shift) % array.shape[longest]
        spots.append(tuple(where))
    return array.at[spots[0]].set(low).at[spots[1]].set(largest)


def block_levels(key, shape, cuts, smallest, high):
    def one(position, shards_of):
        draws = jax.random.uniform(jax.random.fold_in(jax.random.fold_in(key, 6), position), (shards_of,), jnp.float32, smallest / len(cuts), high / len(cuts))
        return jnp.repeat(jnp.exp(draws), shape[position] // shards_of).reshape((-1,) + (1,) * (len(shape) - position - 1))

    loudness = one(*cuts[0])
    for cut in cuts[1:]:
        loudness = loudness * one(*cut)
    return loudness


def assign_block(key, own, number, rows, count, top, bound, lean):
    order = jax.random.permutation(key, count)
    crowded, ordinary = load_shares(count, rows * top, bound, lean, True), load_shares(count, rows * top, bound, lean, False)
    places = jnp.arange(count)

    def named(tallies, rotation):
        used = int((tallies > 0).sum())
        fixed = max(1, used // 4)
        moved = fixed + (places - fixed + rotation * (used - fixed)) % max(1, count - fixed)
        return jnp.zeros((count,), jnp.int32).at[order[jnp.where(places < fixed, places, moved)]].set(jnp.asarray(tallies, jnp.int32))

    tallies = jnp.where(number % 4 == 0, named(crowded, number // 4), named(ordinary, number - number // 4 - 1))
    mixed = jax.random.permutation(jax.random.fold_in(own, 3), count)
    giver, sink = mixed[0:count // 2 * 2:2], mixed[1:count // 2 * 2:2]
    room = jnp.minimum(tallies[giver] - 1, bound - tallies[sink]) // 2
    room = jnp.where((giver == order[0]) | (sink == order[0]) | (tallies[sink] == 0), 0, jnp.maximum(room, 0))
    moved = jax.random.randint(jax.random.fold_in(own, 4), (count // 2,), 0, 1 << 20) % (room + 1)
    tallies = tallies.at[giver].add(-moved).at[sink].add(moved)
    items = jnp.searchsorted(jnp.cumsum(tallies), jnp.arange(rows * top), side="right").astype(jnp.int32)
    listing = items.reshape(top, rows).T
    listing = listing[jax.random.permutation(jax.random.fold_in(own, 1), rows)]
    rotation = jax.random.randint(jax.random.fold_in(own, 2), (rows, 1), 0, top)
    return jnp.take_along_axis(listing, (jnp.arange(top)[None, :] + rotation) % top, axis=1)


def load_shares(number_of, total, reach, lean, full):
    loads = [(1 << 20) // math.isqrt(grade ** lean) + 1 for grade in range(1, number_of + 1)]
    largest = reach if full else min(reach, max(-(-total // number_of), total * loads[0] // sum(loads)))
    least = 1 if total - largest >= number_of - 1 else 0
    counts, surplus = [largest] + [least] * (number_of - 1), total - largest - least * (number_of - 1)
    while surplus > 0:
        candidates = [i for i in range(1, number_of) if counts[i] < largest] or [i for i in range(1, number_of) if counts[i] < reach]
        pool, remaining = sum([loads[i] for i in candidates]), surplus
        for i in candidates:
            addition = min(reach - counts[i], max(1, remaining * loads[i] // pool), surplus)
            counts[i] = counts[i] + addition
            surplus = surplus - addition
    return np.array(counts)


def scatter_about(stream_key, extent, width, most, cuts=(), kind=jnp.bfloat16):
    array = jax.random.normal(stream_key, extent, jnp.float32) * width
    if len(cuts) > 0:
        array = block_levels(stream_key, extent, cuts, -0.22, 0.18) * array
    return jnp.clip(array, min=-most, max=most).astype(kind)


def setup_inputs(seed: int = 0) -> dict:
    key_list = jax.random.split(jax.random.key(seed), 10)
    tokens = scatter_about(key_list[0], (TOKENS, D), 1.0, 6.0, ((0, 64),))
    routes_keys = jax.random.split(jax.random.fold_in(key_list[1], 1), TOKENS // TOK_DEV)
    routes_turns = jax.random.permutation(jax.random.fold_in(key_list[1], 3), TOKENS // TOK_DEV)
    routes = jax.vmap(lambda own, number: assign_block(jax.random.fold_in(key_list[1], 2), own, number, TOK_DEV, EXPERTS, TOPK, CAP, 2))(routes_keys, routes_turns).reshape((TOKENS, TOPK))
    route_gates = jnp.clip(0.049804688 + 0.4501953 * jax.random.uniform(key_list[2], (TOKENS, TOPK), jnp.float32) ** block_levels(key_list[2], (TOKENS, TOPK), ((0, 64),), -0.2, 0.2), 0.049804688, 0.5).astype(jnp.bfloat16)
    domains = with_ends(jax.random.randint(key_list[3], (TOKENS,), 0, NDOM), jax.random.fold_in(key_list[3], 1), 0, NDOM - 1).astype(jnp.int32)
    domain_weight = jnp.clip(jnp.exp(jax.random.uniform(key_list[4], (NDOM,), jnp.float32, math.log(0.25), math.log(4.0))), 0.25, 4.0)
    targets = scatter_about(key_list[5], (TOKENS, D), 1.0, 6.0, ((0, 64),))
    w_gate = scatter_about(key_list[6], (EXPERTS, D, FF), D ** -0.5, 0.1875, ((0, 64), (2, 8)))
    w_up = scatter_about(key_list[7], (EXPERTS, D, FF), D ** -0.5, 0.1875, ((0, 64), (2, 8)))
    w_down = scatter_about(key_list[8], (EXPERTS, FF, D), FF ** -0.5, 0.1875, ((0, 64), (1, 8)))
    return {"tokens": tokens, "routes": routes, "route_gates": route_gates, "domains": domains, "domain_weight": domain_weight, "targets": targets, "w_gate": w_gate, "w_up": w_up, "w_down": w_down}


def slot_layout(routes, route_gates):
    blocks = TOKENS // TOK_DEV
    per_block = TOK_DEV * TOPK
    flat_routes = routes.reshape(blocks, per_block).astype(jnp.int32)
    onehot = (flat_routes[:, :, None] == jnp.arange(EXPERTS, dtype=jnp.int32)[None, None, :]).astype(jnp.int32)
    places = jnp.sum((jnp.cumsum(onehot, 1) - onehot) * onehot, 2).astype(jnp.int32)
    block_ids = jnp.arange(blocks, dtype=jnp.int32)[:, None]
    slot_ids = (flat_routes * SLOTS + block_ids * CAP + places).astype(jnp.int32).reshape(-1)
    token_ids = (block_ids * TOK_DEV + (jnp.arange(per_block, dtype=jnp.int32) // TOPK)[None, :]).astype(jnp.int32).reshape(-1)
    slot_token = jnp.full((EXPERTS * SLOTS,), TOKENS, jnp.int32).at[slot_ids].set(token_ids)
    slot_gate = jnp.zeros((EXPERTS * SLOTS,), jnp.float32).at[slot_ids].set(route_gates.reshape(-1).astype(jnp.float32))
    return slot_token, slot_gate


def block_sum(pieces):
    return jnp.sum(lax.optimization_barrier(pieces.astype(jnp.bfloat16)).astype(jnp.float32), 0)


def expert_forward(slot_rows, gate_w, up_w, down_w):
    gate_pre = jnp.dot(slot_rows, gate_w, preferred_element_type=jnp.float32)
    up_pre = jnp.dot(slot_rows, up_w, preferred_element_type=jnp.float32)
    hidden = (jax.nn.silu(gate_pre) * up_pre).astype(jnp.bfloat16)
    pieces = jnp.einsum("rsf,sfd->srd", hidden.astype(jnp.float32).reshape(SLOTS, N_DP, FF_DEV),
                        down_w.astype(jnp.float32).reshape(N_DP, FF_DEV, D), precision=lax.Precision.HIGHEST)
    return gate_pre, up_pre, hidden, block_sum(pieces)


def expert_backward(slot_rows, slot_grads, gate_w, up_w, down_w):
    gate_pre, up_pre, hidden, unused = expert_forward(slot_rows, gate_w, up_w, down_w)
    hidden_grad = jnp.dot(slot_grads, down_w.T, preferred_element_type=jnp.float32)
    sigma = jax.nn.sigmoid(gate_pre)
    gate_grad = (hidden_grad * up_pre * sigma * (1.0 + gate_pre * (1.0 - sigma))).astype(jnp.bfloat16)
    up_grad = (hidden_grad * gate_pre * sigma).astype(jnp.bfloat16)
    grad_down = jnp.dot(hidden.T, slot_grads, preferred_element_type=jnp.float32)
    grad_gate = jnp.dot(slot_rows.T, gate_grad, preferred_element_type=jnp.float32)
    grad_up = jnp.dot(slot_rows.T, up_grad, preferred_element_type=jnp.float32)
    gate_part = jnp.einsum("rsf,dsf->srd", gate_grad.astype(jnp.float32).reshape(SLOTS, N_DP, FF_DEV),
                           gate_w.astype(jnp.float32).reshape(D, N_DP, FF_DEV), precision=lax.Precision.HIGHEST)
    up_part = jnp.einsum("rsf,dsf->srd", up_grad.astype(jnp.float32).reshape(SLOTS, N_DP, FF_DEV),
                         up_w.astype(jnp.float32).reshape(D, N_DP, FF_DEV), precision=lax.Precision.HIGHEST)
    return grad_gate, grad_up, grad_down, block_sum(gate_part + up_part)


def reference(tokens, routes, route_gates, domains, domain_weight, targets, w_gate, w_up, w_down):
    slot_token, slot_gate = slot_layout(routes, route_gates)
    padded = jnp.concatenate([tokens, jnp.zeros((1, D), jnp.bfloat16)], 0)
    slot_rows = padded[slot_token].reshape(EXPERTS, SLOTS, D)

    def forward_one(items):
        return expert_forward(items[0], items[1], items[2], items[3])[3]

    slot_out = lax.map(forward_one, (slot_rows, w_gate, w_up, w_down))
    weighted = slot_gate[:, None] * slot_out.reshape(EXPERTS * SLOTS, D)
    layer_out = jax.ops.segment_sum(weighted, slot_token, TOKENS + 1)[:TOKENS]
    scales = domain_weight[domains]
    loss_grad = (scales[:, None] * (layer_out - targets.astype(jnp.float32))).astype(jnp.bfloat16)
    grad_padded = jnp.concatenate([loss_grad.astype(jnp.float32), jnp.zeros((1, D), jnp.float32)], 0)
    slot_grads = (slot_gate[:, None] * grad_padded[slot_token]).astype(jnp.bfloat16).reshape(EXPERTS, SLOTS, D)

    def backward_one(items):
        return expert_backward(items[0], items[1], items[2], items[3], items[4])

    grad_gate, grad_up, grad_down, row_sums = lax.map(backward_one, (slot_rows, slot_grads, w_gate, w_up, w_down))
    grad_tokens = jax.ops.segment_sum(row_sums.reshape(EXPERTS * SLOTS, D), slot_token, TOKENS + 1)[:TOKENS]
    return grad_tokens.astype(jnp.bfloat16), grad_gate, grad_up, grad_down
```

```python
import jax
import jax.numpy as jnp
from jax import lax
from jax.sharding import PartitionSpec as P

CONTRACT_LAST = (((1,), (1,)), ((), ()))
CONTRACT_FIRST = (((0,), (0,)), ((), ()))


def dot(a, b, dims=(((1,), (0,)), ((), ()))):
    return lax.dot_general(a, b, dims, preferred_element_type=jnp.float32)


def tables(routes, route_gates, experts, places, first_place):
    count, top = routes.shape
    expert_ids = lax.broadcasted_iota(jnp.int32, (experts, count), 0)
    routes_t = routes.T
    gates_t = route_gates.T.astype(jnp.float32)
    named = jnp.zeros((experts, count), jnp.float32)
    gates = jnp.zeros((experts, count), jnp.float32)
    for k in range(top):
        hit = routes_t[k][None, :] == expert_ids
        named = named + jnp.where(hit, 1.0, 0.0)
        gates = gates + jnp.where(hit, gates_t[k][None, :], 0.0)
    earlier = (
        lax.broadcasted_iota(jnp.int32, (count, count), 0)
        < lax.broadcasted_iota(jnp.int32, (count, count), 1)
    ).astype(jnp.bfloat16)
    place = dot(named.astype(jnp.bfloat16), earlier).astype(jnp.int32)
    wanted = first_place + lax.broadcasted_iota(jnp.int32, (experts, places, count), 1)
    match = (place[:, None, :] == wanted) & (named[:, None, :] > 0.5)
    select = jnp.where(match, 1.0, 0.0).astype(jnp.bfloat16)
    gated = jnp.where(match, gates[:, None, :], 0.0).astype(jnp.bfloat16)
    return (
        select.reshape(experts * places, count),
        gated.reshape(experts * places, count),
    )


def make_shards(n_dp, experts):
    chips = n_dp // 2
    same_core = [[2 * y + c for y in range(chips)] for c in range(2)]
    swap_pairs = [(d, d ^ 1) for d in range(n_dp)]

    def swap(v):
        return lax.ppermute(v, "dp", swap_pairs)

    def over_experts(v):
        v = v.reshape(experts, v.shape[0] // experts, v.shape[1])
        v = lax.all_to_all(v, "expert", split_axis=0, concat_axis=0, tiled=True)
        return v.reshape(-1, v.shape[2])

    def over_chips(v):
        return lax.all_to_all(
            v, "dp", split_axis=0, concat_axis=0, axis_index_groups=same_core, tiled=True
        )

    def gather_columns(v):
        v = over_chips(jnp.broadcast_to(v[None], (chips,) + v.shape))
        return jnp.concatenate([v[y] for y in range(chips)], 1)

    def scatter_columns(v):
        width = v.shape[1] // chips
        v = jnp.stack([v[:, y * width : (y + 1) * width] for y in range(chips)])
        return jnp.sum(over_chips(v).astype(jnp.float32), 0).astype(jnp.bfloat16)

    def shards(tokens, routes, route_gates, domains, domain_weight, targets, w_gate, w_up, w_down):
        count, width = tokens.shape
        place_half = 8
        device = lax.axis_index("dp")
        chip, core = device // 2, device % 2
        block = width // chips
        select, gated = tables(routes, route_gates, experts, place_half, core * place_half)
        my_tokens = lax.dynamic_slice(tokens, (0, chip * block), (count, block))
        my_targets = lax.dynamic_slice(targets, (0, chip * block), (count, block))
        picks = domains[:, None] == jnp.arange(domain_weight.shape[0], dtype=jnp.int32)[None, :]
        scales = jnp.sum(jnp.where(picks, domain_weight[None, :], 0.0), 1)

        gate_w = jnp.concatenate([w_gate[0], swap(w_gate[0])], 1)
        up_w = jnp.concatenate([w_up[0], swap(w_up[0])], 1)
        down_w = jnp.concatenate([w_down[0], swap(w_down[0])], 0)

        slot_rows = gather_columns(over_experts(dot(select, my_tokens).astype(jnp.bfloat16)))
        gate_pre = dot(slot_rows, gate_w)
        up_pre = dot(slot_rows, up_w)
        sigma = jax.nn.sigmoid(gate_pre)
        hidden = (gate_pre * sigma * up_pre).astype(jnp.bfloat16)
        slot_part = dot(hidden, down_w).astype(jnp.bfloat16)
        returned = over_experts(scatter_columns(slot_part))
        half_out = dot(gated, returned, CONTRACT_FIRST)
        layer_out = half_out + swap(half_out)
        loss_grad = (scales[:, None] * (layer_out - my_targets.astype(jnp.float32))).astype(
            jnp.bfloat16
        )
        slot_grads = gather_columns(over_experts(dot(gated, loss_grad).astype(jnp.bfloat16)))

        hidden_grad = dot(slot_grads, down_w, CONTRACT_LAST)
        gate_grad = (hidden_grad * up_pre * sigma * (1.0 + gate_pre * (1.0 - sigma))).astype(
            jnp.bfloat16
        )
        up_grad = (hidden_grad * gate_pre * sigma).astype(jnp.bfloat16)
        row_part = dot(gate_grad, gate_w, CONTRACT_LAST) + dot(up_grad, up_w, CONTRACT_LAST)
        grad_returned = over_experts(scatter_columns(row_part.astype(jnp.bfloat16)))

        half = w_gate.shape[2]
        grad_down = dot(hidden, slot_grads, CONTRACT_FIRST)
        grad_gate = dot(slot_rows, gate_grad, CONTRACT_FIRST)
        grad_up = dot(slot_rows, up_grad, CONTRACT_FIRST)
        grad_down = grad_down[:half] + swap(grad_down[half:])
        grad_gate = grad_gate[:, :half] + swap(grad_gate[:, half:])
        grad_up = grad_up[:, :half] + swap(grad_up[:, half:])

        half_input = dot(select, grad_returned, CONTRACT_FIRST)
        grad_tokens = gather_columns((half_input + swap(half_input)).astype(jnp.bfloat16))
        return (grad_tokens, grad_gate[None], grad_up[None], grad_down[None])

    return shards


def solution(mesh):
    return jax.shard_map(
        make_shards(mesh.shape["dp"], mesh.shape["expert"]),
        mesh=mesh,
        in_specs=(
            P("expert", None),
            P("expert", None),
            P("expert", None),
            P("expert"),
            P(),
            P("expert", None),
            P("expert", None, "dp"),
            P("expert", None, "dp"),
            P("expert", "dp", None),
        ),
        out_specs=(
            P("expert", None),
            P("expert", None, "dp"),
            P("expert", None, "dp"),
            P("expert", "dp", None),
        ),
        check_vma=False,
    )
```

```python
import jax
import jax.numpy as jnp
from jax import lax
from jax.experimental import pallas as pl
from jax.experimental.pallas import tpu as pltpu
from jax.sharding import Mesh
from jax.sharding import PartitionSpec as P

CONTRACT_LAST = (((1,), (1,)), ((), ()))
CONTRACT_FIRST = (((0,), (0,)), ((), ()))
Y, C, X, Z = 4, 2, 4, 16
PLACES = 4
EXPERTS = X * Z


def dot(a, b, dims=(((1,), (0,)), ((), ()))):
    return lax.dot_general(a, b, dims, preferred_element_type=jnp.float32)


def tables(routes, route_gates, first_place):
    count, top = routes.shape
    expert_ids = lax.broadcasted_iota(jnp.int32, (EXPERTS, count), 0)
    routes_t = routes.T
    gates_t = route_gates.T.astype(jnp.float32)
    named = jnp.zeros((EXPERTS, count), jnp.float32)
    gates = jnp.zeros((EXPERTS, count), jnp.float32)
    for k in range(top):
        hit = routes_t[k][None, :] == expert_ids
        named = named + jnp.where(hit, 1.0, 0.0)
        gates = gates + jnp.where(hit, gates_t[k][None, :], 0.0)
    earlier = (
        lax.broadcasted_iota(jnp.int32, (count, count), 0)
        < lax.broadcasted_iota(jnp.int32, (count, count), 1)
    ).astype(jnp.bfloat16)
    place = dot(named.astype(jnp.bfloat16), earlier).astype(jnp.int32)
    wanted = first_place + lax.broadcasted_iota(jnp.int32, (EXPERTS, PLACES, count), 1)
    match = (place[:, None, :] == wanted) & (named[:, None, :] > 0.5)
    select = jnp.where(match, 1.0, 0.0).astype(jnp.bfloat16)
    gated = jnp.where(match, gates[:, None, :], 0.0).astype(jnp.bfloat16)
    slots = EXPERTS * PLACES
    return select.reshape(slots, count), gated.reshape(slots, count)


def exchange(v, axes):
    return lax.all_to_all(v, axes, split_axis=0, concat_axis=0, tiled=True)


def spread(v, axis, size):
    return exchange(jnp.broadcast_to(v[None], (size,) + v.shape), axis)


def over_experts(v):
    v = exchange(v.reshape(EXPERTS, PLACES, v.shape[1]), ("x", "z"))
    return v.reshape(EXPERTS * PLACES, v.shape[2])


def shift(v, by):
    return lax.ppermute(v, "y", [((y + by) % Y, y) for y in range(Y)])


def total(v):
    return jnp.sum(v.astype(jnp.float32), 0)


SLOTS = EXPERTS * PLACES
WIDTH, UNIT, HALF = 1024, 128, 512
PACKED = WIDTH + Y * UNIT
CUT = PACKED // 2
BLOCK = 2 * UNIT
BF16, F32 = jnp.bfloat16, jnp.float32


def call(body, outs, *args):
    return pl.pallas_call(
        body,
        out_shape=[jax.ShapeDtypeStruct(shape, dtype) for shape, dtype in outs],
        compiler_params=pltpu.CompilerParams(vmem_limit_bytes=48 << 20),
    )(*args)


def pack_body(gate_ref, up_ref, down_ref, out_ref, sems):
    moves = [
        (gate_ref, out_ref.at[pl.ds(0, WIDTH), pl.ds(0, UNIT)]),
        (up_ref, out_ref.at[pl.ds(0, WIDTH), pl.ds(UNIT, UNIT)]),
    ]
    for b in range(Y):
        moves.append(
            (down_ref.at[:, pl.ds(b * BLOCK, BLOCK)], out_ref.at[pl.ds(WIDTH + b * UNIT, UNIT), :])
        )
    copies = [pltpu.make_async_copy(src, dst, sems.at[i]) for i, (src, dst) in enumerate(moves)]
    for copy in copies:
        copy.start()
    for copy in copies:
        copy.wait()


def pack(gate, up, down):
    anywhere = pl.BlockSpec(memory_space=pl.ANY)
    return pl.pallas_call(
        pack_body,
        in_specs=[anywhere] * 3,
        out_specs=anywhere,
        out_shape=jax.ShapeDtypeStruct((PACKED, BLOCK), BF16),
        scratch_shapes=[pltpu.SemaphoreType.DMA((2 + Y,))],
    )(gate, up, down)


def rows_of(refs, start, stop):
    if len(refs) == 1:
        return [(0, refs[0][start:stop, :])]
    found = []
    for ref, low in zip(refs, (0, CUT)):
        first, last = max(start, low), min(stop, low + CUT)
        if first < last:
            found.append((first - start, ref[first - low : last - low, :]))
    return found


def packed_refs(refs):
    own, one, two_low, two_high, three = refs
    return [(own,), (one,), (two_low, two_high), (three,)]


def forward_body(rows_ref, w0, w1, w2a, w2b, w3, part_ref, pre_ref, hidden_ref):
    packed = packed_refs((w0, w1, w2a, w2b, w3))
    hidden = []
    for r in (0, 1, 3, 2):
        pre = jnp.zeros((SLOTS, BLOCK), F32)
        for h in range(C):
            for at, w in rows_of(packed[r], h * HALF, (h + 1) * HALF):
                pre = pre + dot(rows_ref[h, :, at : at + w.shape[0]], w)
        pre_ref[r] = pre
        gate, up = pre[:, :UNIT], pre[:, UNIT:]
        hidden_ref[r] = (gate * jax.nn.sigmoid(gate) * up).astype(BF16)
    for b in range(Y):
        start = WIDTH + b * UNIT
        out = jnp.zeros((SLOTS, BLOCK), F32)
        for r in range(Y):
            [(_, w)] = rows_of(packed[r], start, start + UNIT)
            out = out + dot(hidden_ref[r], w)
        part_ref[b // 2, :, (b % 2) * BLOCK : (b % 2 + 1) * BLOCK] = out.astype(BF16)


def backward_body(grads_ref, pre_ref, w0, w1, w2a, w2b, w3, part_ref, pre_grad_ref):
    packed = packed_refs((w0, w1, w2a, w2b, w3))
    for r in range(Y):
        hidden_grad = jnp.zeros((SLOTS, UNIT), F32)
        for b in range(Y):
            start = WIDTH + b * UNIT
            [(_, w)] = rows_of(packed[r], start, start + UNIT)
            piece = grads_ref[b // 2, :, (b % 2) * BLOCK : (b % 2 + 1) * BLOCK]
            hidden_grad = hidden_grad + dot(piece, w, CONTRACT_LAST)
        gate, up = pre_ref[r, :, :UNIT], pre_ref[r, :, UNIT:]
        sigma = jax.nn.sigmoid(gate)
        pre_grad_ref[r, :, :UNIT] = (hidden_grad * up * sigma * (1.0 + gate * (1.0 - sigma))).astype(BF16)
        pre_grad_ref[r, :, UNIT:] = (hidden_grad * gate * sigma).astype(BF16)
    for start in range(0, WIDTH, BLOCK):
        out = jnp.zeros((SLOTS, BLOCK), F32)
        for r in range(Y):
            [(_, w)] = rows_of(packed[r], start, start + BLOCK)
            out = out + dot(pre_grad_ref[r], w, CONTRACT_LAST)
        h, at = start // HALF, start % HALF
        part_ref[h, :, at : at + BLOCK] = out.astype(BF16)


def weight_grads(rows_ref, grads_ref, pre_grad_ref, hidden_ref, r, start):
    if start < WIDTH:
        h, at = start // HALF, start % HALF
        return dot(rows_ref[h, :, at : at + BLOCK], pre_grad_ref[r], CONTRACT_FIRST)
    b = (start - WIDTH) // UNIT
    found = []
    for block in (b, b + 1):
        piece = grads_ref[block // 2, :, (block % 2) * BLOCK : (block % 2 + 1) * BLOCK]
        found.append(dot(hidden_ref[r], piece, CONTRACT_FIRST))
    return jnp.concatenate(found, 0)


def far_grads_body(rows_ref, grads_ref, pre_grad_ref, hidden_ref, low_ref, high_ref):
    for start in range(0, PACKED, BLOCK):
        value = weight_grads(rows_ref, grads_ref, pre_grad_ref, hidden_ref, 2, start).astype(BF16)
        if start < CUT:
            low_ref[start : start + BLOCK, :] = value
        else:
            high_ref[start - CUT : start - CUT + BLOCK, :] = value


def near_grads_body(rows_ref, grads_ref, pre_grad_ref, hidden_ref, low_ref, high_ref, one_ref, three_ref):
    for start in range(0, PACKED, BLOCK):
        one = weight_grads(rows_ref, grads_ref, pre_grad_ref, hidden_ref, 1, start)
        three = weight_grads(rows_ref, grads_ref, pre_grad_ref, hidden_ref, 3, start)
        if start < CUT:
            one = one + low_ref[start : start + BLOCK, :].astype(F32)
        else:
            three = three + high_ref[start - CUT : start - CUT + BLOCK, :].astype(F32)
        one_ref[start : start + BLOCK, :] = one.astype(BF16)
        three_ref[start : start + BLOCK, :] = three.astype(BF16)


def own_grads_body(rows_ref, grads_ref, pre_grad_ref, hidden_ref, out_ref):
    for start in range(0, PACKED, BLOCK):
        out_ref[start : start + BLOCK, :] = weight_grads(rows_ref, grads_ref, pre_grad_ref, hidden_ref, 0, start)


def finish_body(own_ref, before_ref, after_ref, gate_ref, up_ref, down_ref):
    for start in range(0, PACKED, BLOCK):
        rows = slice(start, start + BLOCK)
        value = own_ref[rows, :] + before_ref[rows, :].astype(F32) + after_ref[rows, :].astype(F32)
        if start < WIDTH:
            gate_ref[rows, :] = value[:, :UNIT]
            up_ref[rows, :] = value[:, UNIT:]
        else:
            b = (start - WIDTH) // UNIT
            down_ref[:, b * BLOCK : (b + 1) * BLOCK] = value[:UNIT]
            down_ref[:, (b + 1) * BLOCK : (b + 2) * BLOCK] = value[UNIT:]


def shards(tokens, routes, route_gates, domains, domain_weight, targets, w_gate, w_up, w_down):
    count, width = tokens.shape
    chip, core = lax.axis_index("y"), lax.axis_index("c")

    own = pack(w_gate[0], w_up[0], w_down[0])
    one, three = shift(own, 1), shift(own, -1)
    weights = (own, one, shift(one[:CUT], 1), shift(three[CUT:], -1), three)

    select, gated = tables(routes, route_gates, chip * PLACES)
    my_tokens = lax.dynamic_slice(tokens, (0, core * HALF), (count, HALF))
    my_targets = lax.dynamic_slice(targets, (0, core * HALF), (count, HALF))
    picks = domains[:, None] == jnp.arange(domain_weight.shape[0], dtype=jnp.int32)[None, :]
    scales = jnp.sum(jnp.where(picks, domain_weight[None, :], 0.0), 1)

    slot_rows = spread(over_experts(dot(select, my_tokens).astype(BF16)), "c", C)
    halves, quarters = (C, SLOTS, HALF), (Y, SLOTS, BLOCK)
    slot_part, pre, hidden = call(
        forward_body, [(halves, BF16), (quarters, F32), ((Y, SLOTS, UNIT), BF16)], slot_rows, *weights
    )
    returned = over_experts(total(exchange(slot_part, "c")).astype(BF16))
    quarter_out = dot(gated, returned, CONTRACT_FIRST).astype(BF16)
    layer_out = total(spread(quarter_out, "y", Y))
    loss_grad = (scales[:, None] * (layer_out - my_targets.astype(F32))).astype(BF16)
    slot_grads = spread(over_experts(dot(gated, loss_grad).astype(BF16)), "c", C)

    row_part, pre_grad = call(backward_body, [(halves, BF16), (quarters, BF16)], slot_grads, pre, *weights)
    grad_returned = over_experts(total(exchange(row_part, "c")).astype(BF16))

    saved = (slot_rows, slot_grads, pre_grad, hidden)
    low, high = call(far_grads_body, [((CUT, BLOCK), BF16)] * 2, *saved)
    [own_grads] = call(own_grads_body, [((PACKED, BLOCK), F32)], *saved)
    to_next, to_last = call(near_grads_body, [((PACKED, BLOCK), BF16)] * 2, *saved, shift(low, -1), shift(high, 1))
    quarter_input = dot(select, grad_returned, CONTRACT_FIRST).astype(BF16)
    my_grad = total(spread(quarter_input, "y", Y)).astype(BF16)
    other = lax.ppermute(my_grad, "c", [(0, 1), (1, 0)])
    grad_tokens = jnp.where(core == 0, jnp.concatenate([my_grad, other], 1), jnp.concatenate([other, my_grad], 1))

    own_grads, _ = lax.optimization_barrier((own_grads, my_grad))
    outs = [((WIDTH, UNIT), F32), ((WIDTH, UNIT), F32), ((UNIT, WIDTH), F32)]
    grad_gate, grad_up, grad_down = call(finish_body, outs, own_grads, shift(to_next, -1), shift(to_last, 1))
    return (grad_tokens, grad_gate[None], grad_up[None], grad_down[None])


def solution(mesh):
    fine = Mesh(mesh.devices.reshape(Y, C, X, Z), ("y", "c", "x", "z"))
    expert, dp = ("x", "z"), ("y", "c")
    return jax.shard_map(
        shards,
        mesh=fine,
        in_specs=(
            P(expert, None),
            P(expert, None),
            P(expert, None),
            P(expert),
            P(),
            P(expert, None),
            P(expert, None, dp),
            P(expert, None, dp),
            P(expert, dp, None),
        ),
        out_specs=(
            P(expert, None),
            P(expert, None, dp),
            P(expert, None, dp),
            P(expert, dp, None),
        ),
        check_vma=False,
    )
```

```python
import jax
import jax.numpy as jnp
from jax import lax
from jax.experimental import pallas as pl
from jax.experimental.pallas import tpu as pltpu
from jax.sharding import Mesh
from jax.sharding import PartitionSpec as P

CONTRACT_LAST = (((1,), (1,)), ((), ()))
CONTRACT_FIRST = (((0,), (0,)), ((), ()))
Y, C, X, Z = 4, 2, 4, 16
PLACES = 4
EXPERTS = X * Z


def dot(a, b, dims=(((1,), (0,)), ((), ()))):
    return lax.dot_general(a, b, dims, preferred_element_type=jnp.float32)


def tables(routes, route_gates, first_place):
    count, top = routes.shape
    expert_ids = lax.broadcasted_iota(jnp.int32, (EXPERTS, count), 0)
    routes_t = routes.T
    gates_t = route_gates.T.astype(jnp.float32)
    named = jnp.zeros((EXPERTS, count), jnp.float32)
    gates = jnp.zeros((EXPERTS, count), jnp.float32)
    for k in range(top):
        hit = routes_t[k][None, :] == expert_ids
        named = named + jnp.where(hit, 1.0, 0.0)
        gates = gates + jnp.where(hit, gates_t[k][None, :], 0.0)
    earlier = (
        lax.broadcasted_iota(jnp.int32, (count, count), 0)
        < lax.broadcasted_iota(jnp.int32, (count, count), 1)
    ).astype(jnp.bfloat16)
    place = dot(named.astype(jnp.bfloat16), earlier).astype(jnp.int32)
    wanted = first_place + lax.broadcasted_iota(jnp.int32, (EXPERTS, PLACES, count), 1)
    match = (place[:, None, :] == wanted) & (named[:, None, :] > 0.5)
    select = jnp.where(match, 1.0, 0.0).astype(jnp.bfloat16)
    gated = jnp.where(match, gates[:, None, :], 0.0).astype(jnp.bfloat16)
    slots = EXPERTS * PLACES
    return select.reshape(slots, count), gated.reshape(slots, count)


def exchange(v, axes):
    return lax.all_to_all(v, axes, split_axis=0, concat_axis=0, tiled=True)


def spread(v, axis, size):
    return exchange(jnp.broadcast_to(v[None], (size,) + v.shape), axis)


def over_experts(v):
    v = exchange(v.reshape(EXPERTS, PLACES, v.shape[1]), ("x", "z"))
    return v.reshape(EXPERTS * PLACES, v.shape[2])


def swap(v):
    return lax.ppermute(v, "c", [(0, 1), (1, 0)])


def near(v):
    moves = [(C * ((y + 1) % Y), C * y) for y in range(Y)]
    moves += [(C * y + 1, C * ((y + 1) % Y) + 1) for y in range(Y)]
    return lax.ppermute(v, ("y", "c"), moves)


def far(v):
    return lax.ppermute(v, ("y", "c"), [(C * y + 1, C * ((y + 2) % Y) + 1) for y in range(Y)])


def shift(v, by):
    return lax.ppermute(v, "y", [((y + by) % Y, y) for y in range(Y)])


def total(v):
    return jnp.sum(v.astype(jnp.float32), 0)


SLOTS = EXPERTS * PLACES
WIDTH, UNIT, HALF = 1024, 128, 512
PACKED = WIDTH + Y * UNIT
CUT = PACKED // 2
BLOCK = 2 * UNIT
BF16, F32 = jnp.bfloat16, jnp.float32


def call(body, outs, *args, scratch=()):
    in_smem = {0: pl.BlockSpec(memory_space=pltpu.SMEM)} if args[0].dtype == jnp.int32 else {}
    in_vmem = pl.BlockSpec(memory_space=pltpu.VMEM)
    return pl.pallas_call(
        body,
        in_specs=[in_smem.get(i, in_vmem) for i in range(len(args))],
        out_shape=[jax.ShapeDtypeStruct(shape, dtype) for shape, dtype in outs],
        scratch_shapes=list(scratch),
        compiler_params=pltpu.CompilerParams(vmem_limit_bytes=20 << 20),
    )(*args)


def pack_body(gate_ref, up_ref, down_ref, out_ref, sems):
    moves = [
        (gate_ref, out_ref.at[pl.ds(0, WIDTH), pl.ds(0, UNIT)]),
        (up_ref, out_ref.at[pl.ds(0, WIDTH), pl.ds(UNIT, UNIT)]),
    ]
    for b in range(Y):
        moves.append(
            (down_ref.at[:, pl.ds(b * BLOCK, BLOCK)], out_ref.at[pl.ds(WIDTH + b * UNIT, UNIT), :])
        )
    copies = [pltpu.make_async_copy(src, dst, sems.at[i]) for i, (src, dst) in enumerate(moves)]
    for copy in copies:
        copy.start()
    for copy in copies:
        copy.wait()


def pack(gate, up, down):
    anywhere = pl.BlockSpec(memory_space=pl.ANY)
    return pl.pallas_call(
        pack_body,
        in_specs=[anywhere] * 3,
        out_shape=jax.ShapeDtypeStruct((PACKED, BLOCK), BF16),
        scratch_shapes=[pltpu.SemaphoreType.DMA((2 + Y,))],
    )(gate, up, down)


def rows_of(refs, start, stop):
    if len(refs) == 1:
        return [(0, refs[0][start:stop, :])]
    found = []
    for ref, low in zip(refs, (0, CUT)):
        first, last = max(start, low), min(stop, low + CUT)
        if first < last:
            found.append((first - start, ref[first - low : last - low, :]))
    return found


def packed_refs(refs):
    own, one, two_low, two_high, three = refs
    return [(own,), (one,), (two_low, two_high), (three,)]


def forward_body(rows_ref, w0, w1, w2a, w2b, w3, part_ref, pre_ref):
    packed = packed_refs((w0, w1, w2a, w2b, w3))
    hidden = [None] * Y
    for r in (0, 1, 3, 2):
        pre = jnp.zeros((SLOTS, BLOCK), F32)
        for h in range(C):
            for at, w in rows_of(packed[r], h * HALF, (h + 1) * HALF):
                pre = pre + dot(rows_ref[h, :, at : at + w.shape[0]], w)
        pre_ref[r] = pre
        gate, up = pre[:, :UNIT], pre[:, UNIT:]
        hidden[r] = (gate * jax.nn.sigmoid(gate) * up).astype(BF16)
    for b in range(Y):
        start = WIDTH + b * UNIT
        out = jnp.zeros((SLOTS, BLOCK), F32)
        for r in range(Y):
            [(_, w)] = rows_of(packed[r], start, start + UNIT)
            out = out + dot(hidden[r], w)
        part_ref[b // 2, :, (b % 2) * BLOCK : (b % 2 + 1) * BLOCK] = out.astype(BF16)


def pre_grad_of(pre, hidden_grad):
    gate, up = pre[:, :UNIT], pre[:, UNIT:]
    sigma = jax.nn.sigmoid(gate)
    gate_grad = hidden_grad * up * sigma * (1.0 + gate * (1.0 - sigma))
    up_grad = hidden_grad * gate * sigma
    return jnp.concatenate([gate_grad, up_grad], 1).astype(BF16)


def backward_body(grads_ref, pre_ref, w0, w1, w2a, w2b, w3, part_ref):
    packed = packed_refs((w0, w1, w2a, w2b, w3))
    pre_grads = []
    for r in range(Y):
        hidden_grad = jnp.zeros((SLOTS, UNIT), F32)
        for b in range(Y):
            start = WIDTH + b * UNIT
            [(_, w)] = rows_of(packed[r], start, start + UNIT)
            piece = grads_ref[b // 2, :, (b % 2) * BLOCK : (b % 2 + 1) * BLOCK]
            hidden_grad = hidden_grad + dot(piece, w, CONTRACT_LAST)
        pre_grads.append(pre_grad_of(pre_ref[r], hidden_grad))
    for start in range(0, WIDTH, BLOCK):
        out = jnp.zeros((SLOTS, BLOCK), F32)
        for r in range(Y):
            [(_, w)] = rows_of(packed[r], start, start + BLOCK)
            out = out + dot(pre_grads[r], w, CONTRACT_LAST)
        h, at = start // HALF, start % HALF
        part_ref[h, :, at : at + BLOCK] = out.astype(BF16)


def block_of(ref, b):
    return ref[b // 2, :, (b % 2) * BLOCK : (b % 2 + 1) * BLOCK]


def again_body(core_ref, own_ref, near_ref, far_ref, w_own, w_other, pre_ref, hidden_ref, first_ref):
    first_ref[...] = jnp.where(core_ref[0] == 0, own_ref[...], far_ref[...])
    for g, rows_ref in enumerate((first_ref, near_ref)):
        for k, w in enumerate((w_own, w_other)):
            pre = dot(rows_ref[0], w[:HALF, :]) + dot(rows_ref[1], w[HALF:WIDTH, :])
            pre_ref[g, k] = pre
            gate, up = pre[:, :UNIT], pre[:, UNIT:]
            hidden_ref[g, k] = (gate * jax.nn.sigmoid(gate) * up).astype(BF16)


def weight_grads_body(
    core_ref, own_ref, near_ref, far_ref, rows0_ref, rows1_ref, pre_ref, hidden_ref, w_own, w_other,
    mine_ref, theirs_ref, first_ref,
):
    first_ref[...] = jnp.where(core_ref[0] == 0, own_ref[...], far_ref[...])
    grads, rows = (first_ref, near_ref), (rows0_ref, rows1_ref)
    for k, (w, out_ref) in enumerate(((w_own, mine_ref), (w_other, theirs_ref))):
        pre_grads = []
        for g in range(2):
            hidden_grad = jnp.zeros((SLOTS, UNIT), F32)
            for b in range(Y):
                down = w[WIDTH + b * UNIT : WIDTH + (b + 1) * UNIT, :]
                hidden_grad = hidden_grad + dot(block_of(grads[g], b), down, CONTRACT_LAST)
            pre_grads.append(pre_grad_of(pre_ref[g, k], hidden_grad))
        for b in range(Y):
            out_ref[b * BLOCK : (b + 1) * BLOCK, :] = sum(
                dot(block_of(rows[g], b), pre_grads[g], CONTRACT_FIRST) for g in range(2)
            )
            out_ref[WIDTH + b * UNIT : WIDTH + (b + 1) * UNIT, :] = sum(
                dot(hidden_ref[g, k], block_of(grads[g], b), CONTRACT_FIRST) for g in range(2)
            )


def finish_body(own_ref, other_ref, gate_ref, up_ref, down_ref):
    for start in range(0, PACKED, BLOCK):
        rows = slice(start, start + BLOCK)
        value = own_ref[rows, :] + other_ref[rows, :]
        if start < WIDTH:
            gate_ref[rows, :] = value[:, :UNIT]
            up_ref[rows, :] = value[:, UNIT:]
        else:
            b = (start - WIDTH) // UNIT
            down_ref[:, b * BLOCK : (b + 1) * BLOCK] = value[:UNIT]
            down_ref[:, (b + 1) * BLOCK : (b + 2) * BLOCK] = value[UNIT:]


def shards(tokens, routes, route_gates, domains, domain_weight, targets, w_gate, w_up, w_down):
    count, width = tokens.shape
    chip, core = lax.axis_index("y"), lax.axis_index("c")

    own = pack(w_gate[0], w_up[0], w_down[0])
    one, three = shift(own, 1), shift(own, -1)
    weights = (own, one, shift(one[:CUT], 1), shift(three[CUT:], -1), three)

    select, gated = tables(routes, route_gates, chip * PLACES)
    my_tokens = lax.dynamic_slice(tokens, (0, core * HALF), (count, HALF))
    my_targets = lax.dynamic_slice(targets, (0, core * HALF), (count, HALF))
    picks = domains[:, None] == jnp.arange(domain_weight.shape[0], dtype=jnp.int32)[None, :]
    scales = jnp.sum(jnp.where(picks, domain_weight[None, :], 0.0), 1)

    slot_rows = spread(over_experts(dot(select, my_tokens).astype(BF16)), "c", C)
    halves, quarters = (C, SLOTS, HALF), (Y, SLOTS, BLOCK)
    slot_part, pre = call(forward_body, [(halves, BF16), (quarters, F32)], slot_rows, *weights)
    returned = over_experts(total(exchange(slot_part, "c")).astype(BF16))

    core_id = core.reshape(1).astype(jnp.int32)
    others, near_rows = swap(own), near(slot_rows)
    outs = [((2, 2, SLOTS, BLOCK), F32), ((2, 2, SLOTS, UNIT), BF16), (halves, BF16)]
    again = call(again_body, outs, core_id, slot_rows, near_rows, far(slot_rows), own, others)

    quarter_out = dot(gated, returned, CONTRACT_FIRST).astype(BF16)
    layer_out = total(spread(quarter_out, "y", Y))
    loss_grad = (scales[:, None] * (layer_out - my_targets.astype(F32))).astype(BF16)
    half_grads = over_experts(dot(gated, loss_grad).astype(BF16))
    half_grads, (pre_again, hidden_again, first_rows) = lax.optimization_barrier((half_grads, tuple(again)))
    slot_grads = spread(half_grads, "c", C)

    [row_part] = call(backward_body, [(halves, BF16)], slot_grads, pre, *weights)
    row_sums = total(exchange(row_part, "c")).astype(BF16)
    row_sums, late_grads = lax.optimization_barrier((row_sums, slot_grads))
    grad_returned = over_experts(row_sums)

    mine, theirs = call(
        weight_grads_body, [((PACKED, BLOCK), F32)] * 2,
        core_id, slot_grads, near(late_grads), far(late_grads), first_rows, near_rows, pre_again, hidden_again, own, others,
        scratch=[pltpu.VMEM(halves, BF16)],
    )
    outs = [((WIDTH, UNIT), F32), ((WIDTH, UNIT), F32), ((UNIT, WIDTH), F32)]
    grad_gate, grad_up, grad_down = call(finish_body, outs, mine, swap(theirs))

    quarter_input = dot(select, grad_returned, CONTRACT_FIRST).astype(BF16)
    my_grad = total(spread(quarter_input, "y", Y)).astype(BF16)
    other = swap(my_grad)
    grad_tokens = jnp.where(core == 0, jnp.concatenate([my_grad, other], 1), jnp.concatenate([other, my_grad], 1))
    return (grad_tokens, grad_gate[None], grad_up[None], grad_down[None])


def solution(mesh):
    fine = Mesh(mesh.devices.reshape(Y, C, X, Z), ("y", "c", "x", "z"))
    expert, dp = ("x", "z"), ("y", "c")
    return jax.shard_map(
        shards,
        mesh=fine,
        in_specs=(
            P(expert, None),
            P(expert, None),
            P(expert, None),
            P(expert),
            P(),
            P(expert, None),
            P(expert, None, dp),
            P(expert, None, dp),
            P(expert, dp, None),
        ),
        out_specs=(
            P(expert, None),
            P(expert, None, dp),
            P(expert, None, dp),
            P(expert, dp, None),
        ),
        check_vma=False,
    )
```

```python
import jax
import jax.numpy as jnp
from jax import lax
from jax.experimental import pallas as pl
from jax.experimental.pallas import tpu as pltpu
from jax.sharding import Mesh
from jax.sharding import PartitionSpec as P

CONTRACT_LAST = (((1,), (1,)), ((), ()))
CONTRACT_FIRST = (((0,), (0,)), ((), ()))
Y, C, X, Z = 4, 2, 4, 16
PLACES = 4
EXPERTS = X * Z


def dot(a, b, dims=(((1,), (0,)), ((), ()))):
    return lax.dot_general(a, b, dims, preferred_element_type=jnp.float32)


def tables(routes, route_gates, first_place):
    count, top = routes.shape
    expert_ids = lax.broadcasted_iota(jnp.int32, (EXPERTS, count), 0)
    routes_t = routes.T
    gates_t = route_gates.T.astype(jnp.float32)
    named = jnp.zeros((EXPERTS, count), jnp.float32)
    gates = jnp.zeros((EXPERTS, count), jnp.float32)
    for k in range(top):
        hit = routes_t[k][None, :] == expert_ids
        named = named + jnp.where(hit, 1.0, 0.0)
        gates = gates + jnp.where(hit, gates_t[k][None, :], 0.0)
    earlier = (
        lax.broadcasted_iota(jnp.int32, (count, count), 0)
        < lax.broadcasted_iota(jnp.int32, (count, count), 1)
    ).astype(jnp.bfloat16)
    place = dot(named.astype(jnp.bfloat16), earlier).astype(jnp.int32)
    wanted = first_place + lax.broadcasted_iota(jnp.int32, (EXPERTS, PLACES, count), 1)
    match = (place[:, None, :] == wanted) & (named[:, None, :] > 0.5)
    select = jnp.where(match, 1.0, 0.0).astype(jnp.bfloat16)
    gated = jnp.where(match, gates[:, None, :], 0.0).astype(jnp.bfloat16)
    slots = EXPERTS * PLACES
    return select.reshape(slots, count), gated.reshape(slots, count)


def exchange(v, axes):
    return lax.all_to_all(v, axes, split_axis=0, concat_axis=0, tiled=True)


def spread(v, axis, size):
    return exchange(jnp.broadcast_to(v[None], (size,) + v.shape), axis)


def over_experts(v):
    v = exchange(v.reshape(EXPERTS, PLACES, v.shape[1]), ("x", "z"))
    return v.reshape(EXPERTS * PLACES, v.shape[2])


def swap(v):
    return lax.ppermute(v, "c", [(0, 1), (1, 0)])


def near(v):
    moves = [(C * ((y + 1) % Y), C * y) for y in range(Y)]
    moves += [(C * y + 1, C * ((y + 1) % Y) + 1) for y in range(Y)]
    return lax.ppermute(v, ("y", "c"), moves)


def far(v):
    return lax.ppermute(v, ("y", "c"), [(C * y + 1, C * ((y + 2) % Y) + 1) for y in range(Y)])


def shift(v, by):
    return lax.ppermute(v, "y", [((y + by) % Y, y) for y in range(Y)])


def total(v):
    return jnp.sum(v.astype(jnp.float32), 0)


SLOTS = EXPERTS * PLACES
WIDTH, UNIT, HALF = 1024, 128, 512
PACKED = WIDTH + Y * UNIT
CUT = PACKED // 2
BLOCK = 2 * UNIT
BF16, F32 = jnp.bfloat16, jnp.float32


def call(body, outs, *args, scratch=()):
    in_smem = {0: pl.BlockSpec(memory_space=pltpu.SMEM)} if args[0].dtype == jnp.int32 else {}
    in_vmem = pl.BlockSpec(memory_space=pltpu.VMEM)
    return pl.pallas_call(
        body,
        in_specs=[in_smem.get(i, in_vmem) for i in range(len(args))],
        out_shape=[jax.ShapeDtypeStruct(shape, dtype) for shape, dtype in outs],
        scratch_shapes=list(scratch),
        compiler_params=pltpu.CompilerParams(vmem_limit_bytes=20 << 20),
    )(*args)


def pack_body(gate_ref, up_ref, down_ref, out_ref, sems):
    moves = [
        (gate_ref, out_ref.at[pl.ds(0, WIDTH), pl.ds(0, UNIT)]),
        (up_ref, out_ref.at[pl.ds(0, WIDTH), pl.ds(UNIT, UNIT)]),
    ]
    for b in range(Y):
        moves.append(
            (down_ref.at[:, pl.ds(b * BLOCK, BLOCK)], out_ref.at[pl.ds(WIDTH + b * UNIT, UNIT), :])
        )
    copies = [pltpu.make_async_copy(src, dst, sems.at[i]) for i, (src, dst) in enumerate(moves)]
    for copy in copies:
        copy.start()
    for copy in copies:
        copy.wait()


def pack(gate, up, down):
    anywhere = pl.BlockSpec(memory_space=pl.ANY)
    return pl.pallas_call(
        pack_body,
        in_specs=[anywhere] * 3,
        out_shape=jax.ShapeDtypeStruct((PACKED, BLOCK), BF16),
        scratch_shapes=[pltpu.SemaphoreType.DMA((2 + Y,))],
    )(gate, up, down)


def rows_of(refs, start, stop):
    if len(refs) == 1:
        return [(0, refs[0][start:stop, :])]
    found = []
    for ref, low in zip(refs, (0, CUT)):
        first, last = max(start, low), min(stop, low + CUT)
        if first < last:
            found.append((first - start, ref[first - low : last - low, :]))
    return found


def packed_refs(refs):
    own, one, two_low, two_high, three = refs
    return [(own,), (one,), (two_low, two_high), (three,)]


def forward_body(rows_ref, w0, w1, w2a, w2b, w3, part_ref, pre_ref):
    packed = packed_refs((w0, w1, w2a, w2b, w3))
    hidden = [None] * Y
    for r in (0, 1, 3, 2):
        pre = jnp.zeros((SLOTS, BLOCK), F32)
        for h in range(C):
            for at, w in rows_of(packed[r], h * HALF, (h + 1) * HALF):
                pre = pre + dot(rows_ref[h, :, at : at + w.shape[0]], w)
        pre_ref[r] = pre
        gate, up = pre[:, :UNIT], pre[:, UNIT:]
        hidden[r] = (gate * jax.nn.sigmoid(gate) * up).astype(BF16)
    for b in range(Y):
        start = WIDTH + b * UNIT
        out = jnp.zeros((SLOTS, BLOCK), F32)
        for r in range(Y):
            [(_, w)] = rows_of(packed[r], start, start + UNIT)
            out = out + dot(hidden[r], w)
        part_ref[b // 2, :, (b % 2) * BLOCK : (b % 2 + 1) * BLOCK] = out.astype(BF16)


def pre_grad_of(pre, hidden_grad):
    gate, up = pre[:, :UNIT], pre[:, UNIT:]
    sigma = jax.nn.sigmoid(gate)
    gate_grad = hidden_grad * up * sigma * (1.0 + gate * (1.0 - sigma))
    up_grad = hidden_grad * gate * sigma
    return jnp.concatenate([gate_grad, up_grad], 1).astype(BF16)


def backward_body(grads_ref, pre_ref, w0, w1, w2a, w2b, w3, part_ref):
    packed = packed_refs((w0, w1, w2a, w2b, w3))
    pre_grads = []
    for r in range(Y):
        hidden_grad = jnp.zeros((SLOTS, UNIT), F32)
        for b in range(Y):
            start = WIDTH + b * UNIT
            [(_, w)] = rows_of(packed[r], start, start + UNIT)
            piece = grads_ref[b // 2, :, (b % 2) * BLOCK : (b % 2 + 1) * BLOCK]
            hidden_grad = hidden_grad + dot(piece, w, CONTRACT_LAST)
        pre_grads.append(pre_grad_of(pre_ref[r], hidden_grad))
    for start in range(0, WIDTH, BLOCK):
        out = jnp.zeros((SLOTS, BLOCK), F32)
        for r in range(Y):
            [(_, w)] = rows_of(packed[r], start, start + BLOCK)
            out = out + dot(pre_grads[r], w, CONTRACT_LAST)
        h, at = start // HALF, start % HALF
        part_ref[h, :, at : at + BLOCK] = out.astype(BF16)


def block_of(ref, b):
    return ref[b // 2, :, (b % 2) * BLOCK : (b % 2 + 1) * BLOCK]


def again_body(core_ref, own_ref, near_ref, far_ref, w_own, w_other, pre_ref, hidden_ref, first_ref):
    first_ref[...] = jnp.where(core_ref[0] == 0, own_ref[...], far_ref[...])
    for g, rows_ref in enumerate((first_ref, near_ref)):
        for k, w in enumerate((w_own, w_other)):
            pre = dot(rows_ref[0], w[:HALF, :]) + dot(rows_ref[1], w[HALF:WIDTH, :])
            pre_ref[g, k] = pre
            gate, up = pre[:, :UNIT], pre[:, UNIT:]
            hidden_ref[g, k] = (gate * jax.nn.sigmoid(gate) * up).astype(BF16)


def weight_grads_body(
    core_ref, own_ref, near_ref, far_ref, rows0_ref, rows1_ref, pre_ref, hidden_ref, w_own, w_other,
    mine_ref, theirs_ref, first_ref,
):
    first_ref[...] = jnp.where(core_ref[0] == 0, own_ref[...], far_ref[...])
    grads, rows = (first_ref, near_ref), (rows0_ref, rows1_ref)
    for k, (w, out_ref) in enumerate(((w_own, mine_ref), (w_other, theirs_ref))):
        pre_grads = []
        for g in range(2):
            hidden_grad = jnp.zeros((SLOTS, UNIT), F32)
            for b in range(Y):
                down = w[WIDTH + b * UNIT : WIDTH + (b + 1) * UNIT, :]
                hidden_grad = hidden_grad + dot(block_of(grads[g], b), down, CONTRACT_LAST)
            pre_grads.append(pre_grad_of(pre_ref[g, k], hidden_grad))
        for b in range(Y):
            out_ref[b * BLOCK : (b + 1) * BLOCK, :] = sum(
                dot(block_of(rows[g], b), pre_grads[g], CONTRACT_FIRST) for g in range(2)
            ).astype(out_ref.dtype)
            out_ref[WIDTH + b * UNIT : WIDTH + (b + 1) * UNIT, :] = sum(
                dot(hidden_ref[g, k], block_of(grads[g], b), CONTRACT_FIRST) for g in range(2)
            ).astype(out_ref.dtype)


def finish_body(own_ref, other_ref, gate_ref, up_ref, down_ref):
    for start in range(0, PACKED, BLOCK):
        rows = slice(start, start + BLOCK)
        value = own_ref[rows, :] + other_ref[rows, :].astype(F32)
        if start < WIDTH:
            gate_ref[rows, :] = value[:, :UNIT]
            up_ref[rows, :] = value[:, UNIT:]
        else:
            b = (start - WIDTH) // UNIT
            down_ref[:, b * BLOCK : (b + 1) * BLOCK] = value[:UNIT]
            down_ref[:, (b + 1) * BLOCK : (b + 2) * BLOCK] = value[UNIT:]


def shards(tokens, routes, route_gates, domains, domain_weight, targets, w_gate, w_up, w_down):
    count, width = tokens.shape
    chip, core = lax.axis_index("y"), lax.axis_index("c")

    own = pack(w_gate[0], w_up[0], w_down[0])
    one, three = shift(own, 1), shift(own, -1)
    weights = (own, one, shift(one[:CUT], 1), shift(three[CUT:], -1), three)

    select, gated = tables(routes, route_gates, chip * PLACES)
    my_tokens = lax.dynamic_slice(tokens, (0, core * HALF), (count, HALF))
    my_targets = lax.dynamic_slice(targets, (0, core * HALF), (count, HALF))
    picks = domains[:, None] == jnp.arange(domain_weight.shape[0], dtype=jnp.int32)[None, :]
    scales = jnp.sum(jnp.where(picks, domain_weight[None, :], 0.0), 1)

    slot_rows = spread(over_experts(dot(select, my_tokens).astype(BF16)), "c", C)
    halves, quarters = (C, SLOTS, HALF), (Y, SLOTS, BLOCK)
    slot_part, pre = call(forward_body, [(halves, BF16), (quarters, F32)], slot_rows, *weights)
    returned = over_experts(total(exchange(slot_part, "c")).astype(BF16))

    core_id = core.reshape(1).astype(jnp.int32)
    others, near_rows = swap(own), near(slot_rows)
    outs = [((2, 2, SLOTS, BLOCK), F32), ((2, 2, SLOTS, UNIT), BF16), (halves, BF16)]
    again = call(again_body, outs, core_id, slot_rows, near_rows, far(slot_rows), own, others)

    quarter_out = dot(gated, returned, CONTRACT_FIRST).astype(BF16)
    layer_out = total(spread(quarter_out, "y", Y))
    loss_grad = (scales[:, None] * (layer_out - my_targets.astype(F32))).astype(BF16)
    loss_grad, (pre_again, hidden_again, first_rows) = lax.optimization_barrier((loss_grad, tuple(again)))
    slot_grads = spread(over_experts(dot(gated, loss_grad).astype(BF16)), "c", C)

    [row_part] = call(backward_body, [(halves, BF16)], slot_grads, pre, *weights)
    row_sums = total(exchange(row_part, "c")).astype(BF16)
    row_sums, late_grads = lax.optimization_barrier((row_sums, slot_grads))
    grad_returned = over_experts(row_sums)

    mine, theirs = call(
        weight_grads_body, [((PACKED, BLOCK), F32), ((PACKED, BLOCK), BF16)],
        core_id, slot_grads, near(late_grads), far(late_grads), first_rows, near_rows, pre_again, hidden_again, own, others,
        scratch=[pltpu.VMEM(halves, BF16)],
    )
    outs = [((WIDTH, UNIT), F32), ((WIDTH, UNIT), F32), ((UNIT, WIDTH), F32)]
    grad_gate, grad_up, grad_down = call(finish_body, outs, mine, swap(theirs))

    quarter_input = dot(select, grad_returned, CONTRACT_FIRST).astype(BF16)
    my_grad = total(spread(quarter_input, "y", Y)).astype(BF16)
    other = swap(my_grad)
    grad_tokens = jnp.where(core == 0, jnp.concatenate([my_grad, other], 1), jnp.concatenate([other, my_grad], 1))
    return (grad_tokens, grad_gate[None], grad_up[None], grad_down[None])


def solution(mesh):
    fine = Mesh(mesh.devices.reshape(Y, C, X, Z), ("y", "c", "x", "z"))
    expert, dp = ("x", "z"), ("y", "c")
    return jax.shard_map(
        shards,
        mesh=fine,
        in_specs=(
            P(expert, None),
            P(expert, None),
            P(expert, None),
            P(expert),
            P(),
            P(expert, None),
            P(expert, None, dp),
            P(expert, None, dp),
            P(expert, dp, None),
        ),
        out_specs=(
            P(expert, None),
            P(expert, None, dp),
            P(expert, None, dp),
            P(expert, dp, None),
        ),
        check_vma=False,
    )
```

```python
import jax
import jax.numpy as jnp
from jax import lax
from jax.experimental import pallas as pl
from jax.experimental.pallas import tpu as pltpu
from jax.sharding import Mesh
from jax.sharding import PartitionSpec as P

CONTRACT_LAST = (((1,), (1,)), ((), ()))
CONTRACT_FIRST = (((0,), (0,)), ((), ()))
Y, C, X, Z = 4, 2, 4, 16
PLACES = 4
EXPERTS = X * Z


def dot(a, b, dims=(((1,), (0,)), ((), ()))):
    return lax.dot_general(a, b, dims, preferred_element_type=jnp.float32)


def tables(routes, route_gates, first_place):
    count, top = routes.shape
    expert_ids = lax.broadcasted_iota(jnp.int32, (EXPERTS, count), 0)
    routes_t = routes.T
    gates_t = route_gates.T.astype(jnp.float32)
    named = jnp.zeros((EXPERTS, count), jnp.float32)
    gates = jnp.zeros((EXPERTS, count), jnp.float32)
    for k in range(top):
        hit = routes_t[k][None, :] == expert_ids
        named = named + jnp.where(hit, 1.0, 0.0)
        gates = gates + jnp.where(hit, gates_t[k][None, :], 0.0)
    earlier = (
        lax.broadcasted_iota(jnp.int32, (count, count), 0)
        < lax.broadcasted_iota(jnp.int32, (count, count), 1)
    ).astype(jnp.bfloat16)
    place = dot(named.astype(jnp.bfloat16), earlier).astype(jnp.int32)
    wanted = first_place + lax.broadcasted_iota(jnp.int32, (EXPERTS, PLACES, count), 1)
    match = (place[:, None, :] == wanted) & (named[:, None, :] > 0.5)
    select = jnp.where(match, 1.0, 0.0).astype(jnp.bfloat16)
    gated = jnp.where(match, gates[:, None, :], 0.0).astype(jnp.bfloat16)
    slots = EXPERTS * PLACES
    return select.reshape(slots, count), gated.reshape(slots, count)


def exchange(v, axes):
    return lax.all_to_all(v, axes, split_axis=0, concat_axis=0, tiled=True)


def spread(v, axis, size):
    return exchange(jnp.broadcast_to(v[None], (size,) + v.shape), axis)


def over_experts(v):
    v = exchange(v.reshape(EXPERTS, PLACES, v.shape[1]), ("x", "z"))
    return v.reshape(EXPERTS * PLACES, v.shape[2])


def swap(v):
    return lax.ppermute(v, "c", [(0, 1), (1, 0)])


def near(v):
    moves = [(C * ((y + 1) % Y), C * y) for y in range(Y)]
    moves += [(C * y + 1, C * ((y + 1) % Y) + 1) for y in range(Y)]
    return lax.ppermute(v, ("y", "c"), moves)


def far(v):
    return lax.ppermute(v, ("y", "c"), [(C * y + 1, C * ((y + 2) % Y) + 1) for y in range(Y)])


def shift(v, by):
    return lax.ppermute(v, "y", [((y + by) % Y, y) for y in range(Y)])


def total(v):
    return jnp.sum(v.astype(jnp.float32), 0)


SLOTS = EXPERTS * PLACES
WIDTH, UNIT, HALF = 1024, 128, 512
PACKED = WIDTH + Y * UNIT
CUT = PACKED // 2
BLOCK = 2 * UNIT
BF16, F32 = jnp.bfloat16, jnp.float32


def call(body, outs, *args, scratch=()):
    in_smem = {0: pl.BlockSpec(memory_space=pltpu.SMEM)} if args[0].dtype == jnp.int32 else {}
    in_vmem = pl.BlockSpec(memory_space=pltpu.VMEM)
    return pl.pallas_call(
        body,
        in_specs=[in_smem.get(i, in_vmem) for i in range(len(args))],
        out_shape=[jax.ShapeDtypeStruct(shape, dtype) for shape, dtype in outs],
        scratch_shapes=list(scratch),
        compiler_params=pltpu.CompilerParams(vmem_limit_bytes=20 << 20),
    )(*args)


def pack_body(gate_ref, up_ref, down_ref, out_ref, sems):
    moves = [
        (gate_ref, out_ref.at[pl.ds(0, WIDTH), pl.ds(0, UNIT)]),
        (up_ref, out_ref.at[pl.ds(0, WIDTH), pl.ds(UNIT, UNIT)]),
    ]
    for b in range(Y):
        moves.append(
            (down_ref.at[:, pl.ds(b * BLOCK, BLOCK)], out_ref.at[pl.ds(WIDTH + b * UNIT, UNIT), :])
        )
    copies = [pltpu.make_async_copy(src, dst, sems.at[i]) for i, (src, dst) in enumerate(moves)]
    for copy in copies:
        copy.start()
    for copy in copies:
        copy.wait()


def pack(gate, up, down):
    anywhere = pl.BlockSpec(memory_space=pl.ANY)
    return pl.pallas_call(
        pack_body,
        in_specs=[anywhere] * 3,
        out_shape=jax.ShapeDtypeStruct((PACKED, BLOCK), BF16),
        scratch_shapes=[pltpu.SemaphoreType.DMA((2 + Y,))],
    )(gate, up, down)


def rows_of(refs, start, stop):
    if len(refs) == 1:
        return [(0, refs[0][start:stop, :])]
    found = []
    for ref, low in zip(refs, (0, CUT)):
        first, last = max(start, low), min(stop, low + CUT)
        if first < last:
            found.append((first - start, ref[first - low : last - low, :]))
    return found


def packed_refs(refs):
    own, one, two_low, two_high, three = refs
    return [(own,), (one,), (two_low, two_high), (three,)]


def part(core_ref, blocks, keep_ref, send_ref):
    for i in range(2):
        low, high = blocks[i].astype(BF16), blocks[2 + i].astype(BF16)
        keep_ref[:, i * BLOCK : (i + 1) * BLOCK] = jnp.where(core_ref[0] == 0, low, high)
        send_ref[:, i * BLOCK : (i + 1) * BLOCK] = jnp.where(core_ref[0] == 0, high, low)


def forward_body(core_ref, rows_ref, w0, w1, w2a, w2b, w3, keep_ref, send_ref, pre_ref):
    packed = packed_refs((w0, w1, w2a, w2b, w3))
    blocks = []
    hidden = [None] * Y
    for r in (0, 1, 3, 2):
        pre = jnp.zeros((SLOTS, BLOCK), F32)
        for h in range(C):
            for at, w in rows_of(packed[r], h * HALF, (h + 1) * HALF):
                pre = pre + dot(rows_ref[h, :, at : at + w.shape[0]], w)
        pre_ref[r] = pre
        gate, up = pre[:, :UNIT], pre[:, UNIT:]
        hidden[r] = (gate * jax.nn.sigmoid(gate) * up).astype(BF16)
    for b in range(Y):
        start = WIDTH + b * UNIT
        out = jnp.zeros((SLOTS, BLOCK), F32)
        for r in range(Y):
            [(_, w)] = rows_of(packed[r], start, start + UNIT)
            out = out + dot(hidden[r], w)
        blocks.append(out)
    part(core_ref, blocks, keep_ref, send_ref)


def pre_grad_of(pre, hidden_grad):
    gate, up = pre[:, :UNIT], pre[:, UNIT:]
    sigma = jax.nn.sigmoid(gate)
    gate_grad = hidden_grad * up * sigma * (1.0 + gate * (1.0 - sigma))
    up_grad = hidden_grad * gate * sigma
    return jnp.concatenate([gate_grad, up_grad], 1).astype(BF16)


def backward_body(core_ref, grads_ref, pre_ref, w0, w1, w2a, w2b, w3, keep_ref, send_ref):
    blocks = []
    packed = packed_refs((w0, w1, w2a, w2b, w3))
    pre_grads = []
    for r in range(Y):
        hidden_grad = jnp.zeros((SLOTS, UNIT), F32)
        for b in range(Y):
            start = WIDTH + b * UNIT
            [(_, w)] = rows_of(packed[r], start, start + UNIT)
            piece = grads_ref[b // 2, :, (b % 2) * BLOCK : (b % 2 + 1) * BLOCK]
            hidden_grad = hidden_grad + dot(piece, w, CONTRACT_LAST)
        pre_grads.append(pre_grad_of(pre_ref[r], hidden_grad))
    for start in range(0, WIDTH, BLOCK):
        out = jnp.zeros((SLOTS, BLOCK), F32)
        for r in range(Y):
            [(_, w)] = rows_of(packed[r], start, start + BLOCK)
            out = out + dot(pre_grads[r], w, CONTRACT_LAST)
        blocks.append(out)
    part(core_ref, blocks, keep_ref, send_ref)


def block_of(ref, b):
    return ref[b // 2, :, (b % 2) * BLOCK : (b % 2 + 1) * BLOCK]


def again_body(core_ref, own_ref, near_ref, far_ref, w_own, w_other, pre_ref, hidden_ref, first_ref):
    first_ref[...] = jnp.where(core_ref[0] == 0, own_ref[...], far_ref[...])
    for g, rows_ref in enumerate((first_ref, near_ref)):
        for k, w in enumerate((w_own, w_other)):
            pre = dot(rows_ref[0], w[:HALF, :]) + dot(rows_ref[1], w[HALF:WIDTH, :])
            pre_ref[g, k] = pre
            gate, up = pre[:, :UNIT], pre[:, UNIT:]
            hidden_ref[g, k] = (gate * jax.nn.sigmoid(gate) * up).astype(BF16)


def weight_grads_body(
    core_ref, own_ref, near_ref, far_ref, rows0_ref, rows1_ref, pre_ref, hidden_ref, w_own, w_other,
    mine_ref, theirs_ref, first_ref,
):
    first_ref[...] = jnp.where(core_ref[0] == 0, own_ref[...], far_ref[...])
    grads, rows = (first_ref, near_ref), (rows0_ref, rows1_ref)
    for k, (w, out_ref) in enumerate(((w_own, mine_ref), (w_other, theirs_ref))):
        pre_grads = []
        for g in range(2):
            hidden_grad = jnp.zeros((SLOTS, UNIT), F32)
            for b in range(Y):
                down = w[WIDTH + b * UNIT : WIDTH + (b + 1) * UNIT, :]
                hidden_grad = hidden_grad + dot(block_of(grads[g], b), down, CONTRACT_LAST)
            pre_grads.append(pre_grad_of(pre_ref[g, k], hidden_grad))
        for b in range(Y):
            out_ref[b * BLOCK : (b + 1) * BLOCK, :] = sum(
                dot(block_of(rows[g], b), pre_grads[g], CONTRACT_FIRST) for g in range(2)
            ).astype(out_ref.dtype)
            out_ref[WIDTH + b * UNIT : WIDTH + (b + 1) * UNIT, :] = sum(
                dot(hidden_ref[g, k], block_of(grads[g], b), CONTRACT_FIRST) for g in range(2)
            ).astype(out_ref.dtype)


def finish_body(own_ref, other_ref, gate_ref, up_ref, down_ref):
    for start in range(0, PACKED, BLOCK):
        rows = slice(start, start + BLOCK)
        value = own_ref[rows, :] + other_ref[rows, :].astype(F32)
        if start < WIDTH:
            gate_ref[rows, :] = value[:, :UNIT]
            up_ref[rows, :] = value[:, UNIT:]
        else:
            b = (start - WIDTH) // UNIT
            down_ref[:, b * BLOCK : (b + 1) * BLOCK] = value[:UNIT]
            down_ref[:, (b + 1) * BLOCK : (b + 2) * BLOCK] = value[UNIT:]


def shards(tokens, routes, route_gates, domains, domain_weight, targets, w_gate, w_up, w_down):
    count, width = tokens.shape
    chip, core = lax.axis_index("y"), lax.axis_index("c")

    own = pack(w_gate[0], w_up[0], w_down[0])
    one, three = shift(own, 1), shift(own, -1)
    weights = (own, one, shift(one[:CUT], 1), shift(three[CUT:], -1), three)

    select, gated = tables(routes, route_gates, chip * PLACES)
    my_tokens = lax.dynamic_slice(tokens, (0, core * HALF), (count, HALF))
    my_targets = lax.dynamic_slice(targets, (0, core * HALF), (count, HALF))
    picks = domains[:, None] == jnp.arange(domain_weight.shape[0], dtype=jnp.int32)[None, :]
    scales = jnp.sum(jnp.where(picks, domain_weight[None, :], 0.0), 1)

    core_id = core.reshape(1).astype(jnp.int32)
    half, halves, quarters = (SLOTS, HALF), (C, SLOTS, HALF), (Y, SLOTS, BLOCK)
    slot_rows = spread(over_experts(dot(select, my_tokens).astype(BF16)), "c", C)
    keep, send, pre = call(forward_body, [(half, BF16), (half, BF16), (quarters, F32)], core_id, slot_rows, *weights)
    returned = over_experts((keep.astype(F32) + swap(send).astype(F32)).astype(BF16))

    others, near_rows = swap(own), near(slot_rows)
    outs = [((2, 2, SLOTS, BLOCK), F32), ((2, 2, SLOTS, UNIT), BF16), (halves, BF16)]
    again = call(again_body, outs, core_id, slot_rows, near_rows, far(slot_rows), own, others)

    quarter_out = dot(gated, returned, CONTRACT_FIRST).astype(BF16)
    layer_out = total(spread(quarter_out, "y", Y))
    loss_grad = (scales[:, None] * (layer_out - my_targets.astype(F32))).astype(BF16)
    loss_grad, (pre_again, hidden_again, first_rows) = lax.optimization_barrier((loss_grad, tuple(again)))
    slot_grads = spread(over_experts(dot(gated, loss_grad).astype(BF16)), "c", C)
    keep, send = call(backward_body, [(half, BF16), (half, BF16)], core_id, slot_grads, pre, *weights)
    row_sums = (keep.astype(F32) + swap(send).astype(F32)).astype(BF16)
    row_sums, late_grads = lax.optimization_barrier((row_sums, slot_grads))
    grad_returned = over_experts(row_sums)

    mine, theirs = call(
        weight_grads_body, [((PACKED, BLOCK), F32), ((PACKED, BLOCK), BF16)],
        core_id, slot_grads, near(late_grads), far(late_grads), first_rows, near_rows, pre_again, hidden_again, own, others,
        scratch=[pltpu.VMEM(halves, BF16)],
    )
    outs = [((WIDTH, UNIT), F32), ((WIDTH, UNIT), F32), ((UNIT, WIDTH), F32)]
    grad_gate, grad_up, grad_down = call(finish_body, outs, mine, swap(theirs))

    quarter_input = dot(select, grad_returned, CONTRACT_FIRST).astype(BF16)
    my_grad = total(spread(quarter_input, "y", Y)).astype(BF16)
    other = swap(my_grad)
    grad_tokens = jnp.where(core == 0, jnp.concatenate([my_grad, other], 1), jnp.concatenate([other, my_grad], 1))
    return (grad_tokens, grad_gate[None], grad_up[None], grad_down[None])


def solution(mesh):
    fine = Mesh(mesh.devices.reshape(Y, C, X, Z), ("y", "c", "x", "z"))
    expert, dp = ("x", "z"), ("y", "c")
    return jax.shard_map(
        shards,
        mesh=fine,
        in_specs=(
            P(expert, None),
            P(expert, None),
            P(expert, None),
            P(expert),
            P(),
            P(expert, None),
            P(expert, None, dp),
            P(expert, None, dp),
            P(expert, dp, None),
        ),
        out_specs=(
            P(expert, None),
            P(expert, None, dp),
            P(expert, None, dp),
            P(expert, dp, None),
        ),
        check_vma=False,
    )
```

```python
import jax
import jax.numpy as jnp
from jax import lax
from jax.experimental import pallas as pl
from jax.experimental.pallas import tpu as pltpu
from jax.sharding import Mesh
from jax.sharding import PartitionSpec as P

CONTRACT_LAST = (((1,), (1,)), ((), ()))
CONTRACT_FIRST = (((0,), (0,)), ((), ()))
Y, C, X, Z = 4, 2, 4, 16
PLACES = 4
EXPERTS = X * Z


def dot(a, b, dims=(((1,), (0,)), ((), ()))):
    return lax.dot_general(a, b, dims, preferred_element_type=jnp.float32)


def tables(routes, route_gates, first_place):
    count, top = routes.shape
    expert_ids = lax.broadcasted_iota(jnp.int32, (EXPERTS, count), 0)
    routes_t = routes.T
    gates_t = route_gates.T.astype(jnp.float32)
    named = jnp.zeros((EXPERTS, count), jnp.float32)
    gates = jnp.zeros((EXPERTS, count), jnp.float32)
    for k in range(top):
        hit = routes_t[k][None, :] == expert_ids
        named = named + jnp.where(hit, 1.0, 0.0)
        gates = gates + jnp.where(hit, gates_t[k][None, :], 0.0)
    earlier = (
        lax.broadcasted_iota(jnp.int32, (count, count), 0)
        < lax.broadcasted_iota(jnp.int32, (count, count), 1)
    ).astype(jnp.bfloat16)
    place = dot(named.astype(jnp.bfloat16), earlier).astype(jnp.int32)
    wanted = first_place + lax.broadcasted_iota(jnp.int32, (EXPERTS, PLACES, count), 1)
    match = (place[:, None, :] == wanted) & (named[:, None, :] > 0.5)
    select = jnp.where(match, 1.0, 0.0).astype(jnp.bfloat16)
    gated = jnp.where(match, gates[:, None, :], 0.0).astype(jnp.bfloat16)
    slots = EXPERTS * PLACES
    return select.reshape(slots, count), gated.reshape(slots, count)


def exchange(v, axes):
    return lax.all_to_all(v, axes, split_axis=0, concat_axis=0, tiled=True)


def spread(v, axis, size):
    return exchange(jnp.broadcast_to(v[None], (size,) + v.shape), axis)


def over_experts(v):
    v = exchange(v.reshape(EXPERTS, PLACES, v.shape[1]), ("x", "z"))
    return v.reshape(EXPERTS * PLACES, v.shape[2])


def swap(v):
    return lax.ppermute(v, "c", [(0, 1), (1, 0)])


def near(v):
    moves = [(C * ((y + 1) % Y), C * y) for y in range(Y)]
    moves += [(C * y + 1, C * ((y + 1) % Y) + 1) for y in range(Y)]
    return lax.ppermute(v, ("y", "c"), moves)


def far(v):
    return lax.ppermute(v, ("y", "c"), [(C * y + 1, C * ((y + 2) % Y) + 1) for y in range(Y)])


def shift(v, by):
    return lax.ppermute(v, "y", [((y + by) % Y, y) for y in range(Y)])


def total(v):
    return jnp.sum(v.astype(jnp.float32), 0)


SLOTS = EXPERTS * PLACES
WIDTH, UNIT, HALF = 1024, 128, 512
PACKED = WIDTH + Y * UNIT
CUT = PACKED // 2
BLOCK = 2 * UNIT
BF16, F32 = jnp.bfloat16, jnp.float32


def call(body, outs, *args, scratch=()):
    in_smem = {0: pl.BlockSpec(memory_space=pltpu.SMEM)} if args[0].dtype == jnp.int32 else {}
    in_vmem = pl.BlockSpec(memory_space=pltpu.VMEM)
    return pl.pallas_call(
        body,
        in_specs=[in_smem.get(i, in_vmem) for i in range(len(args))],
        out_shape=[jax.ShapeDtypeStruct(shape, dtype) for shape, dtype in outs],
        scratch_shapes=list(scratch),
        compiler_params=pltpu.CompilerParams(vmem_limit_bytes=20 << 20),
    )(*args)


def pack_body(gate_ref, up_ref, down_ref, out_ref, sems):
    moves = [
        (gate_ref, out_ref.at[pl.ds(0, WIDTH), pl.ds(0, UNIT)]),
        (up_ref, out_ref.at[pl.ds(0, WIDTH), pl.ds(UNIT, UNIT)]),
    ]
    for b in range(Y):
        moves.append(
            (down_ref.at[:, pl.ds(b * BLOCK, BLOCK)], out_ref.at[pl.ds(WIDTH + b * UNIT, UNIT), :])
        )
    copies = [pltpu.make_async_copy(src, dst, sems.at[i]) for i, (src, dst) in enumerate(moves)]
    for copy in copies:
        copy.start()
    for copy in copies:
        copy.wait()


def pack(gate, up, down):
    anywhere = pl.BlockSpec(memory_space=pl.ANY)
    return pl.pallas_call(
        pack_body,
        in_specs=[anywhere] * 3,
        out_shape=jax.ShapeDtypeStruct((PACKED, BLOCK), BF16),
        scratch_shapes=[pltpu.SemaphoreType.DMA((2 + Y,))],
    )(gate, up, down)


def rows_of(refs, start, stop):
    if len(refs) == 1:
        return [(0, refs[0][start:stop, :])]
    found = []
    for ref, low in zip(refs, (0, CUT)):
        first, last = max(start, low), min(stop, low + CUT)
        if first < last:
            found.append((first - start, ref[first - low : last - low, :]))
    return found


def packed_refs(refs):
    own, one, two_low, two_high, three = refs
    return [(own,), (one,), (two_low, two_high), (three,)]


def part(core_ref, blocks, keep_ref, send_ref):
    for i in range(2):
        low, high = blocks[i].astype(BF16), blocks[2 + i].astype(BF16)
        keep_ref[:, i * BLOCK : (i + 1) * BLOCK] = jnp.where(core_ref[0] == 0, low, high)
        send_ref[:, i * BLOCK : (i + 1) * BLOCK] = jnp.where(core_ref[0] == 0, high, low)


def forward_body(core_ref, rows_ref, w0, w1, w2a, w2b, w3, keep_ref, send_ref, pre_ref):
    packed = packed_refs((w0, w1, w2a, w2b, w3))
    blocks = []
    hidden = [None] * Y
    for r in (0, 1, 3, 2):
        pre = jnp.zeros((SLOTS, BLOCK), F32)
        for h in range(C):
            for at, w in rows_of(packed[r], h * HALF, (h + 1) * HALF):
                pre = pre + dot(rows_ref[h, :, at : at + w.shape[0]], w)
        pre_ref[r] = pre
        gate, up = pre[:, :UNIT], pre[:, UNIT:]
        hidden[r] = (gate * jax.nn.sigmoid(gate) * up).astype(BF16)
    for b in range(Y):
        start = WIDTH + b * UNIT
        out = jnp.zeros((SLOTS, BLOCK), F32)
        for r in range(Y):
            [(_, w)] = rows_of(packed[r], start, start + UNIT)
            out = out + dot(hidden[r], w)
        blocks.append(out)
    part(core_ref, blocks, keep_ref, send_ref)


def pre_grad_of(pre, hidden_grad):
    gate, up = pre[:, :UNIT], pre[:, UNIT:]
    sigma = jax.nn.sigmoid(gate)
    gate_grad = hidden_grad * up * sigma * (1.0 + gate * (1.0 - sigma))
    up_grad = hidden_grad * gate * sigma
    return jnp.concatenate([gate_grad, up_grad], 1).astype(BF16)


def backward_body(core_ref, grads_ref, pre_ref, w0, w1, w2a, w2b, w3, keep_ref, send_ref):
    blocks = []
    packed = packed_refs((w0, w1, w2a, w2b, w3))
    pre_grads = []
    for r in range(Y):
        hidden_grad = jnp.zeros((SLOTS, UNIT), F32)
        for b in range(Y):
            start = WIDTH + b * UNIT
            [(_, w)] = rows_of(packed[r], start, start + UNIT)
            piece = grads_ref[b // 2, :, (b % 2) * BLOCK : (b % 2 + 1) * BLOCK]
            hidden_grad = hidden_grad + dot(piece, w, CONTRACT_LAST)
        pre_grads.append(pre_grad_of(pre_ref[r], hidden_grad))
    for start in range(0, WIDTH, BLOCK):
        out = jnp.zeros((SLOTS, BLOCK), F32)
        for r in range(Y):
            [(_, w)] = rows_of(packed[r], start, start + BLOCK)
            out = out + dot(pre_grads[r], w, CONTRACT_LAST)
        blocks.append(out)
    part(core_ref, blocks, keep_ref, send_ref)


def block_of(ref, b):
    return ref[b // 2, :, (b % 2) * BLOCK : (b % 2 + 1) * BLOCK]


def again_body(core_ref, own_ref, near_ref, far_ref, w_own, w_other, pre_ref, hidden_ref, first_ref):
    first_ref[...] = jnp.where(core_ref[0] == 0, own_ref[...], far_ref[...])
    for g, rows_ref in enumerate((first_ref, near_ref)):
        for k, w in enumerate((w_own, w_other)):
            pre = dot(rows_ref[0], w[:HALF, :]) + dot(rows_ref[1], w[HALF:WIDTH, :])
            pre_ref[g, k] = pre
            gate, up = pre[:, :UNIT], pre[:, UNIT:]
            hidden_ref[g, k] = (gate * jax.nn.sigmoid(gate) * up).astype(BF16)


def weight_grads_body(
    core_ref, own_ref, near_ref, far_ref, rows0_ref, rows1_ref, pre_ref, hidden_ref, w_own, w_other,
    mine_ref, theirs_ref, first_ref,
):
    first_ref[...] = jnp.where(core_ref[0] == 0, own_ref[...], far_ref[...])
    grads, rows = (first_ref, near_ref), (rows0_ref, rows1_ref)
    for k, (w, out_ref) in enumerate(((w_own, mine_ref), (w_other, theirs_ref))):
        pre_grads = []
        for g in range(2):
            hidden_grad = jnp.zeros((SLOTS, UNIT), F32)
            for b in range(Y):
                down = w[WIDTH + b * UNIT : WIDTH + (b + 1) * UNIT, :]
                hidden_grad = hidden_grad + dot(block_of(grads[g], b), down, CONTRACT_LAST)
            pre_grads.append(pre_grad_of(pre_ref[g, k], hidden_grad))
        for b in range(Y):
            out_ref[b * BLOCK : (b + 1) * BLOCK, :] = sum(
                dot(block_of(rows[g], b), pre_grads[g], CONTRACT_FIRST) for g in range(2)
            ).astype(out_ref.dtype)
            out_ref[WIDTH + b * UNIT : WIDTH + (b + 1) * UNIT, :] = sum(
                dot(hidden_ref[g, k], block_of(grads[g], b), CONTRACT_FIRST) for g in range(2)
            ).astype(out_ref.dtype)


def loss_body(parts_ref, targets_ref, scales_ref, gated_ref, out_ref):
    layer_out = parts_ref[0].astype(F32)
    for y in range(1, Y):
        layer_out = layer_out + parts_ref[y].astype(F32)
    loss_grad = (scales_ref[...] * (layer_out - targets_ref[...].astype(F32))).astype(BF16)
    out_ref[...] = dot(gated_ref[...], loss_grad).astype(BF16)


def finish_body(own_ref, other_ref, gate_ref, up_ref, down_ref):
    for start in range(0, PACKED, BLOCK):
        rows = slice(start, start + BLOCK)
        value = own_ref[rows, :] + other_ref[rows, :].astype(F32)
        if start < WIDTH:
            gate_ref[rows, :] = value[:, :UNIT]
            up_ref[rows, :] = value[:, UNIT:]
        else:
            b = (start - WIDTH) // UNIT
            down_ref[:, b * BLOCK : (b + 1) * BLOCK] = value[:UNIT]
            down_ref[:, (b + 1) * BLOCK : (b + 2) * BLOCK] = value[UNIT:]


def shards(tokens, routes, route_gates, domains, domain_weight, targets, w_gate, w_up, w_down):
    count, width = tokens.shape
    chip, core = lax.axis_index("y"), lax.axis_index("c")

    own = pack(w_gate[0], w_up[0], w_down[0])
    one, three = shift(own, 1), shift(own, -1)
    weights = (own, one, shift(one[:CUT], 1), shift(three[CUT:], -1), three)

    select, gated = tables(routes, route_gates, chip * PLACES)
    my_tokens = lax.dynamic_slice(tokens, (0, core * HALF), (count, HALF))
    my_targets = lax.dynamic_slice(targets, (0, core * HALF), (count, HALF))
    picks = domains[:, None] == jnp.arange(domain_weight.shape[0], dtype=jnp.int32)[None, :]
    scales = jnp.sum(jnp.where(picks, domain_weight[None, :], 0.0), 1)

    core_id = core.reshape(1).astype(jnp.int32)
    half, halves, quarters = (SLOTS, HALF), (C, SLOTS, HALF), (Y, SLOTS, BLOCK)
    slot_rows = spread(over_experts(dot(select, my_tokens).astype(BF16)), "c", C)
    keep, send, pre = call(forward_body, [(half, BF16), (half, BF16), (quarters, F32)], core_id, slot_rows, *weights)
    returned = over_experts((keep.astype(F32) + swap(send).astype(F32)).astype(BF16))

    others, near_rows, far_rows = swap(own), near(slot_rows), far(slot_rows)
    quarter_out = dot(gated, returned, CONTRACT_FIRST).astype(BF16)
    parts = spread(quarter_out, "y", Y)
    parts, others, near_rows, far_rows = lax.optimization_barrier((parts, others, near_rows, far_rows))
    [sent] = call(loss_body, [(half, BF16)], parts, my_targets, scales[:, None], gated)
    slot_grads = spread(over_experts(sent), "c", C)
    keep, send = call(backward_body, [(half, BF16), (half, BF16)], core_id, slot_grads, pre, *weights)
    row_sums = (keep.astype(F32) + swap(send).astype(F32)).astype(BF16)
    row_sums, late_grads, late_rows = lax.optimization_barrier((row_sums, slot_grads, slot_rows))
    grad_returned = over_experts(row_sums)

    outs = [((2, 2, SLOTS, BLOCK), F32), ((2, 2, SLOTS, UNIT), BF16), (halves, BF16)]
    pre_again, hidden_again, first_rows = call(
        again_body, outs, core_id, late_rows, near_rows, far_rows, own, others
    )
    mine, theirs = call(
        weight_grads_body, [((PACKED, BLOCK), F32), ((PACKED, BLOCK), BF16)],
        core_id, slot_grads, near(late_grads), far(late_grads), first_rows, near_rows, pre_again, hidden_again, own, others,
        scratch=[pltpu.VMEM(halves, BF16)],
    )
    outs = [((WIDTH, UNIT), F32), ((WIDTH, UNIT), F32), ((UNIT, WIDTH), F32)]
    grad_gate, grad_up, grad_down = call(finish_body, outs, mine, swap(theirs))

    quarter_input = dot(select, grad_returned, CONTRACT_FIRST).astype(BF16)
    my_grad = total(spread(quarter_input, "y", Y)).astype(BF16)
    other = swap(my_grad)
    grad_tokens = jnp.where(core == 0, jnp.concatenate([my_grad, other], 1), jnp.concatenate([other, my_grad], 1))
    return (grad_tokens, grad_gate[None], grad_up[None], grad_down[None])


def solution(mesh):
    fine = Mesh(mesh.devices.reshape(Y, C, X, Z), ("y", "c", "x", "z"))
    expert, dp = ("x", "z"), ("y", "c")
    return jax.shard_map(
        shards,
        mesh=fine,
        in_specs=(
            P(expert, None),
            P(expert, None),
            P(expert, None),
            P(expert),
            P(),
            P(expert, None),
            P(expert, None, dp),
            P(expert, None, dp),
            P(expert, dp, None),
        ),
        out_specs=(
            P(expert, None),
            P(expert, None, dp),
            P(expert, None, dp),
            P(expert, dp, None),
        ),
        check_vma=False,
    )
```

```python
import jax
import jax.numpy as jnp
from jax import lax
from jax.experimental import pallas as pl
from jax.experimental.pallas import tpu as pltpu
from jax.sharding import Mesh
from jax.sharding import PartitionSpec as P

CONTRACT_LAST = (((1,), (1,)), ((), ()))
CONTRACT_FIRST = (((0,), (0,)), ((), ()))
Y, C, X, Z = 4, 2, 4, 16
PLACES = 4
EXPERTS = X * Z


def dot(a, b, dims=(((1,), (0,)), ((), ()))):
    return lax.dot_general(a, b, dims, preferred_element_type=jnp.float32)


def tables(routes, route_gates, first_place):
    count, top = routes.shape
    expert_ids = lax.broadcasted_iota(jnp.int32, (EXPERTS, count), 0)
    routes_t = routes.T
    gates_t = route_gates.T.astype(jnp.float32)
    named = jnp.zeros((EXPERTS, count), jnp.float32)
    gates = jnp.zeros((EXPERTS, count), jnp.float32)
    for k in range(top):
        hit = routes_t[k][None, :] == expert_ids
        named = named + jnp.where(hit, 1.0, 0.0)
        gates = gates + jnp.where(hit, gates_t[k][None, :], 0.0)
    earlier = (
        lax.broadcasted_iota(jnp.int32, (count, count), 0)
        < lax.broadcasted_iota(jnp.int32, (count, count), 1)
    ).astype(jnp.bfloat16)
    place = dot(named.astype(jnp.bfloat16), earlier).astype(jnp.int32)
    wanted = first_place + lax.broadcasted_iota(jnp.int32, (EXPERTS, PLACES, count), 1)
    match = (place[:, None, :] == wanted) & (named[:, None, :] > 0.5)
    select = jnp.where(match, 1.0, 0.0).astype(jnp.bfloat16)
    gated = jnp.where(match, gates[:, None, :], 0.0).astype(jnp.bfloat16)
    slots = EXPERTS * PLACES
    return select.reshape(slots, count), gated.reshape(slots, count)


def exchange(v, axes):
    return lax.all_to_all(v, axes, split_axis=0, concat_axis=0, tiled=True)


def spread(v, axis, size):
    return exchange(jnp.broadcast_to(v[None], (size,) + v.shape), axis)


def over_experts(v):
    v = exchange(v.reshape(EXPERTS, PLACES, v.shape[1]), ("x", "z"))
    return v.reshape(EXPERTS * PLACES, v.shape[2])


def swap(v):
    return lax.ppermute(v, "c", [(0, 1), (1, 0)])


def near(v):
    moves = [(C * ((y + 1) % Y), C * y) for y in range(Y)]
    moves += [(C * y + 1, C * ((y + 1) % Y) + 1) for y in range(Y)]
    return lax.ppermute(v, ("y", "c"), moves)


def far(v):
    return lax.ppermute(v, ("y", "c"), [(C * y + 1, C * ((y + 2) % Y) + 1) for y in range(Y)])


def shift(v, by):
    return lax.ppermute(v, "y", [((y + by) % Y, y) for y in range(Y)])


def total(v):
    return jnp.sum(v.astype(jnp.float32), 0)


SLOTS = EXPERTS * PLACES
WIDTH, UNIT, HALF = 1024, 128, 512
PACKED = WIDTH + Y * UNIT
CUT = PACKED // 2
BLOCK = 2 * UNIT
BF16, F32 = jnp.bfloat16, jnp.float32


def call(body, outs, *args, scratch=()):
    in_smem = {0: pl.BlockSpec(memory_space=pltpu.SMEM)} if args[0].dtype == jnp.int32 else {}
    in_vmem = pl.BlockSpec(memory_space=pltpu.VMEM)
    return pl.pallas_call(
        body,
        in_specs=[in_smem.get(i, in_vmem) for i in range(len(args))],
        out_shape=[jax.ShapeDtypeStruct(shape, dtype) for shape, dtype in outs],
        scratch_shapes=list(scratch),
        compiler_params=pltpu.CompilerParams(vmem_limit_bytes=20 << 20),
    )(*args)


def pack_body(gate_ref, up_ref, down_ref, out_ref, sems):
    moves = [
        (gate_ref, out_ref.at[pl.ds(0, WIDTH), pl.ds(0, UNIT)]),
        (up_ref, out_ref.at[pl.ds(0, WIDTH), pl.ds(UNIT, UNIT)]),
    ]
    for b in range(Y):
        moves.append(
            (down_ref.at[:, pl.ds(b * BLOCK, BLOCK)], out_ref.at[pl.ds(WIDTH + b * UNIT, UNIT), :])
        )
    copies = [pltpu.make_async_copy(src, dst, sems.at[i]) for i, (src, dst) in enumerate(moves)]
    for copy in copies:
        copy.start()
    for copy in copies:
        copy.wait()


def pack(gate, up, down):
    anywhere = pl.BlockSpec(memory_space=pl.ANY)
    return pl.pallas_call(
        pack_body,
        in_specs=[anywhere] * 3,
        out_shape=jax.ShapeDtypeStruct((PACKED, BLOCK), BF16),
        scratch_shapes=[pltpu.SemaphoreType.DMA((2 + Y,))],
    )(gate, up, down)


def rows_of(refs, start, stop):
    if len(refs) == 1:
        return [(0, refs[0][start:stop, :])]
    found = []
    for ref, low in zip(refs, (0, CUT)):
        first, last = max(start, low), min(stop, low + CUT)
        if first < last:
            found.append((first - start, ref[first - low : last - low, :]))
    return found


def packed_refs(refs):
    own, one, two_low, two_high, three = refs
    return [(own,), (one,), (two_low, two_high), (three,)]


def part(core_ref, blocks, keep_ref, send_ref):
    for i in range(2):
        low, high = blocks[i].astype(BF16), blocks[2 + i].astype(BF16)
        keep_ref[:, i * BLOCK : (i + 1) * BLOCK] = jnp.where(core_ref[0] == 0, low, high)
        send_ref[:, i * BLOCK : (i + 1) * BLOCK] = jnp.where(core_ref[0] == 0, high, low)


def forward_body(core_ref, rows_ref, w0, w1, w2a, w2b, w3, keep_ref, send_ref, pre_ref):
    packed = packed_refs((w0, w1, w2a, w2b, w3))
    blocks = []
    hidden = [None] * Y
    for r in (0, 1, 3, 2):
        pre = jnp.zeros((SLOTS, BLOCK), F32)
        for h in range(C):
            for at, w in rows_of(packed[r], h * HALF, (h + 1) * HALF):
                pre = pre + dot(rows_ref[h, :, at : at + w.shape[0]], w)
        pre_ref[r] = pre
        gate, up = pre[:, :UNIT], pre[:, UNIT:]
        hidden[r] = (gate * jax.nn.sigmoid(gate) * up).astype(BF16)
    for b in range(Y):
        start = WIDTH + b * UNIT
        out = jnp.zeros((SLOTS, BLOCK), F32)
        for r in range(Y):
            [(_, w)] = rows_of(packed[r], start, start + UNIT)
            out = out + dot(hidden[r], w)
        blocks.append(out)
    part(core_ref, blocks, keep_ref, send_ref)


def pre_grad_of(pre, hidden_grad):
    gate, up = pre[:, :UNIT], pre[:, UNIT:]
    sigma = jax.nn.sigmoid(gate)
    gate_grad = hidden_grad * up * sigma * (1.0 + gate * (1.0 - sigma))
    up_grad = hidden_grad * gate * sigma
    return jnp.concatenate([gate_grad, up_grad], 1).astype(BF16)


def backward_body(core_ref, grads_ref, pre_ref, w0, w1, w2a, w2b, w3, keep_ref, send_ref):
    blocks = []
    packed = packed_refs((w0, w1, w2a, w2b, w3))
    pre_grads = []
    for r in range(Y):
        hidden_grad = jnp.zeros((SLOTS, UNIT), F32)
        for b in range(Y):
            start = WIDTH + b * UNIT
            [(_, w)] = rows_of(packed[r], start, start + UNIT)
            piece = grads_ref[b // 2, :, (b % 2) * BLOCK : (b % 2 + 1) * BLOCK]
            hidden_grad = hidden_grad + dot(piece, w, CONTRACT_LAST)
        pre_grads.append(pre_grad_of(pre_ref[r], hidden_grad))
    for start in range(0, WIDTH, BLOCK):
        out = jnp.zeros((SLOTS, BLOCK), F32)
        for r in range(Y):
            [(_, w)] = rows_of(packed[r], start, start + BLOCK)
            out = out + dot(pre_grads[r], w, CONTRACT_LAST)
        blocks.append(out)
    part(core_ref, blocks, keep_ref, send_ref)


def block_of(ref, b):
    return ref[b // 2, :, (b % 2) * BLOCK : (b % 2 + 1) * BLOCK]


def again_body(core_ref, own_ref, near_ref, far_ref, w_own, w_other, pre_ref, hidden_ref, first_ref):
    first_ref[...] = jnp.where(core_ref[0] == 0, own_ref[...], far_ref[...])
    for g, rows_ref in enumerate((first_ref, near_ref)):
        for k, w in enumerate((w_own, w_other)):
            pre = dot(rows_ref[0], w[:HALF, :]) + dot(rows_ref[1], w[HALF:WIDTH, :])
            pre_ref[g, k] = pre
            gate, up = pre[:, :UNIT], pre[:, UNIT:]
            hidden_ref[g, k] = (gate * jax.nn.sigmoid(gate) * up).astype(BF16)


def weight_grads_body(
    core_ref, own_ref, near_ref, far_ref, rows0_ref, rows1_ref, pre_ref, hidden_ref, w_own, w_other,
    mine_ref, theirs_ref, first_ref,
):
    first_ref[...] = jnp.where(core_ref[0] == 0, own_ref[...], far_ref[...])
    grads, rows = (first_ref, near_ref), (rows0_ref, rows1_ref)
    for k, (w, out_ref) in enumerate(((w_own, mine_ref), (w_other, theirs_ref))):
        pre_grads = []
        for g in range(2):
            hidden_grad = jnp.zeros((SLOTS, UNIT), F32)
            for b in range(Y):
                down = w[WIDTH + b * UNIT : WIDTH + (b + 1) * UNIT, :]
                hidden_grad = hidden_grad + dot(block_of(grads[g], b), down, CONTRACT_LAST)
            pre_grads.append(pre_grad_of(pre_ref[g, k], hidden_grad))
        for b in range(Y):
            out_ref[b * BLOCK : (b + 1) * BLOCK, :] = sum(
                dot(block_of(rows[g], b), pre_grads[g], CONTRACT_FIRST) for g in range(2)
            ).astype(out_ref.dtype)
            out_ref[WIDTH + b * UNIT : WIDTH + (b + 1) * UNIT, :] = sum(
                dot(hidden_ref[g, k], block_of(grads[g], b), CONTRACT_FIRST) for g in range(2)
            ).astype(out_ref.dtype)


def finish_body(own_ref, other_ref, gate_ref, up_ref, down_ref):
    for start in range(0, PACKED, BLOCK):
        rows = slice(start, start + BLOCK)
        value = own_ref[rows, :] + other_ref[rows, :].astype(F32)
        if start < WIDTH:
            gate_ref[rows, :] = value[:, :UNIT]
            up_ref[rows, :] = value[:, UNIT:]
        else:
            b = (start - WIDTH) // UNIT
            down_ref[:, b * BLOCK : (b + 1) * BLOCK] = value[:UNIT]
            down_ref[:, (b + 1) * BLOCK : (b + 2) * BLOCK] = value[UNIT:]


def shards(tokens, routes, route_gates, domains, domain_weight, targets, w_gate, w_up, w_down):
    count, width = tokens.shape
    chip, core = lax.axis_index("y"), lax.axis_index("c")

    own = pack(w_gate[0], w_up[0], w_down[0])
    one, three = shift(own, 1), shift(own, -1)
    weights = (own, one, shift(one[:CUT], 1), shift(three[CUT:], -1), three)

    select, gated = tables(routes, route_gates, chip * PLACES)
    my_tokens = lax.dynamic_slice(tokens, (0, core * HALF), (count, HALF))
    my_targets = lax.dynamic_slice(targets, (0, core * HALF), (count, HALF))
    picks = domains[:, None] == jnp.arange(domain_weight.shape[0], dtype=jnp.int32)[None, :]
    scales = jnp.sum(jnp.where(picks, domain_weight[None, :], 0.0), 1)

    core_id = core.reshape(1).astype(jnp.int32)
    half, halves, quarters = (SLOTS, HALF), (C, SLOTS, HALF), (Y, SLOTS, BLOCK)
    slot_rows = spread(over_experts(dot(select, my_tokens).astype(BF16)), "c", C)
    keep, send, pre = call(forward_body, [(half, BF16), (half, BF16), (quarters, F32)], core_id, slot_rows, *weights)
    returned = over_experts((keep.astype(F32) + swap(send).astype(F32)).astype(BF16))

    others, near_rows, far_rows = swap(own), near(slot_rows), far(slot_rows)
    quarter_out = dot(gated, returned, CONTRACT_FIRST).astype(BF16)
    quarter_out, others, near_rows, far_rows = lax.optimization_barrier((quarter_out, others, near_rows, far_rows))
    layer_out = total(spread(quarter_out, "y", Y))
    loss_grad = (scales[:, None] * (layer_out - my_targets.astype(F32))).astype(BF16)
    slot_grads = spread(over_experts(dot(gated, loss_grad).astype(BF16)), "c", C)
    keep, send = call(backward_body, [(half, BF16), (half, BF16)], core_id, slot_grads, pre, *weights)
    row_sums = (keep.astype(F32) + swap(send).astype(F32)).astype(BF16)
    row_sums, late_grads, late_rows = lax.optimization_barrier((row_sums, slot_grads, slot_rows))
    grad_returned = over_experts(row_sums)

    outs = [((2, 2, SLOTS, BLOCK), F32), ((2, 2, SLOTS, UNIT), BF16), (halves, BF16)]
    pre_again, hidden_again, first_rows = call(
        again_body, outs, core_id, late_rows, near_rows, far_rows, own, others
    )
    mine, theirs = call(
        weight_grads_body, [((PACKED, BLOCK), F32), ((PACKED, BLOCK), BF16)],
        core_id, slot_grads, near(late_grads), far(late_grads), first_rows, near_rows, pre_again, hidden_again, own, others,
        scratch=[pltpu.VMEM(halves, BF16)],
    )
    outs = [((WIDTH, UNIT), F32), ((WIDTH, UNIT), F32), ((UNIT, WIDTH), F32)]
    grad_gate, grad_up, grad_down = call(finish_body, outs, mine, swap(theirs))

    quarter_input = dot(select, grad_returned, CONTRACT_FIRST).astype(BF16)
    my_grad = total(spread(quarter_input, "y", Y)).astype(BF16)
    other = swap(my_grad)
    grad_tokens = jnp.where(core == 0, jnp.concatenate([my_grad, other], 1), jnp.concatenate([other, my_grad], 1))
    return (grad_tokens, grad_gate[None], grad_up[None], grad_down[None])


def solution(mesh):
    fine = Mesh(mesh.devices.reshape(Y, C, X, Z), ("y", "c", "x", "z"))
    expert, dp = ("x", "z"), ("y", "c")
    return jax.shard_map(
        shards,
        mesh=fine,
        in_specs=(
            P(expert, None),
            P(expert, None),
            P(expert, None),
            P(expert),
            P(),
            P(expert, None),
            P(expert, None, dp),
            P(expert, None, dp),
            P(expert, dp, None),
        ),
        out_specs=(
            P(expert, None),
            P(expert, None, dp),
            P(expert, None, dp),
            P(expert, dp, None),
        ),
        check_vma=False,
    )
```

```python
import jax
import jax.numpy as jnp
from jax import lax
from jax.experimental import pallas as pl
from jax.experimental.pallas import tpu as pltpu
from jax.sharding import Mesh
from jax.sharding import PartitionSpec as P

CONTRACT_LAST = (((1,), (1,)), ((), ()))
CONTRACT_FIRST = (((0,), (0,)), ((), ()))
Y, C, X, Z = 4, 2, 4, 16
PLACES = 4
EXPERTS = X * Z


def dot(a, b, dims=(((1,), (0,)), ((), ()))):
    return lax.dot_general(a, b, dims, preferred_element_type=jnp.float32)


def tables(routes, route_gates, first_place):
    count, top = routes.shape
    expert_ids = lax.broadcasted_iota(jnp.int32, (EXPERTS, count), 0)
    routes_t = routes.T
    gates_t = route_gates.T.astype(jnp.float32)
    named = jnp.zeros((EXPERTS, count), jnp.float32)
    gates = jnp.zeros((EXPERTS, count), jnp.float32)
    for k in range(top):
        hit = routes_t[k][None, :] == expert_ids
        named = named + jnp.where(hit, 1.0, 0.0)
        gates = gates + jnp.where(hit, gates_t[k][None, :], 0.0)
    earlier = (
        lax.broadcasted_iota(jnp.int32, (count, count), 0)
        < lax.broadcasted_iota(jnp.int32, (count, count), 1)
    ).astype(jnp.bfloat16)
    place = dot(named.astype(jnp.bfloat16), earlier).astype(jnp.int32)
    wanted = first_place + lax.broadcasted_iota(jnp.int32, (EXPERTS, PLACES, count), 1)
    match = (place[:, None, :] == wanted) & (named[:, None, :] > 0.5)
    select = jnp.where(match, 1.0, 0.0).astype(jnp.bfloat16)
    gated = jnp.where(match, gates[:, None, :], 0.0).astype(jnp.bfloat16)
    slots = EXPERTS * PLACES
    return select.reshape(slots, count), gated.reshape(slots, count)


def exchange(v, axes):
    return lax.all_to_all(v, axes, split_axis=0, concat_axis=0, tiled=True)


def spread(v, axis, size):
    return exchange(jnp.broadcast_to(v[None], (size,) + v.shape), axis)


def over_experts(v):
    v = exchange(v.reshape(EXPERTS, PLACES, v.shape[1]), ("x", "z"))
    return v.reshape(EXPERTS * PLACES, v.shape[2])


def swap(v):
    return lax.ppermute(v, "c", [(0, 1), (1, 0)])


def near(v):
    moves = [(C * ((y + 1) % Y), C * y) for y in range(Y)]
    moves += [(C * y + 1, C * ((y + 1) % Y) + 1) for y in range(Y)]
    return lax.ppermute(v, ("y", "c"), moves)


def far(v):
    return lax.ppermute(v, ("y", "c"), [(C * y + 1, C * ((y + 2) % Y) + 1) for y in range(Y)])


def shift(v, by):
    return lax.ppermute(v, "y", [((y + by) % Y, y) for y in range(Y)])


def total(v):
    return jnp.sum(v.astype(jnp.float32), 0)


SLOTS = EXPERTS * PLACES
WIDTH, UNIT, HALF = 1024, 128, 512
PACKED = WIDTH + Y * UNIT
CUT = PACKED // 2
BLOCK = 2 * UNIT
BF16, F32 = jnp.bfloat16, jnp.float32


def call(body, outs, *args, scratch=(), away=()):
    in_smem = {0: pl.BlockSpec(memory_space=pltpu.SMEM)} if args[0].dtype == jnp.int32 else {}
    in_vmem = pl.BlockSpec(memory_space=pltpu.VMEM)
    return pl.pallas_call(
        body,
        in_specs=[pl.BlockSpec(memory_space=pl.ANY) if i in away else in_smem.get(i, in_vmem) for i in range(len(args))],
        out_shape=[jax.ShapeDtypeStruct(shape, dtype) for shape, dtype in outs],
        scratch_shapes=list(scratch),
        compiler_params=pltpu.CompilerParams(vmem_limit_bytes=20 << 20),
    )(*args)


def pack_body(gate_ref, up_ref, down_ref, out_ref, sems):
    moves = [
        (gate_ref, out_ref.at[pl.ds(0, WIDTH), pl.ds(0, UNIT)]),
        (up_ref, out_ref.at[pl.ds(0, WIDTH), pl.ds(UNIT, UNIT)]),
    ]
    for b in range(Y):
        moves.append(
            (down_ref.at[:, pl.ds(b * BLOCK, BLOCK)], out_ref.at[pl.ds(WIDTH + b * UNIT, UNIT), :])
        )
    copies = [pltpu.make_async_copy(src, dst, sems.at[i]) for i, (src, dst) in enumerate(moves)]
    for copy in copies:
        copy.start()
    for copy in copies:
        copy.wait()


def pack(gate, up, down):
    anywhere = pl.BlockSpec(memory_space=pl.ANY)
    return pl.pallas_call(
        pack_body,
        in_specs=[anywhere] * 3,
        out_shape=jax.ShapeDtypeStruct((PACKED, BLOCK), BF16),
        scratch_shapes=[pltpu.SemaphoreType.DMA((2 + Y,))],
    )(gate, up, down)


def rows_of(refs, start, stop):
    if len(refs) == 1:
        return [(0, refs[0][start:stop, :])]
    found = []
    for ref, low in zip(refs, (0, CUT)):
        first, last = max(start, low), min(stop, low + CUT)
        if first < last:
            found.append((first - start, ref[first - low : last - low, :]))
    return found


def packed_refs(refs):
    own, one, two_low, two_high, three = refs
    return [(own,), (one,), (two_low, two_high), (three,)]


def part(core_ref, blocks, keep_ref, send_ref):
    for i in range(2):
        low, high = blocks[i].astype(BF16), blocks[2 + i].astype(BF16)
        keep_ref[:, i * BLOCK : (i + 1) * BLOCK] = jnp.where(core_ref[0] == 0, low, high)
        send_ref[:, i * BLOCK : (i + 1) * BLOCK] = jnp.where(core_ref[0] == 0, high, low)


def forward_body(core_ref, rows_ref, w0, w1, w2a, w2b, w3, keep_ref, send_ref, pre_ref):
    packed = packed_refs((w0, w1, w2a, w2b, w3))
    blocks = []
    hidden = [None] * Y
    for r in (0, 1, 3, 2):
        pre = jnp.zeros((SLOTS, BLOCK), F32)
        for h in range(C):
            for at, w in rows_of(packed[r], h * HALF, (h + 1) * HALF):
                pre = pre + dot(rows_ref[h, :, at : at + w.shape[0]], w)
        pre_ref[r] = pre
        gate, up = pre[:, :UNIT], pre[:, UNIT:]
        hidden[r] = (gate * jax.nn.sigmoid(gate) * up).astype(BF16)
    for b in range(Y):
        start = WIDTH + b * UNIT
        out = jnp.zeros((SLOTS, BLOCK), F32)
        for r in range(Y):
            [(_, w)] = rows_of(packed[r], start, start + UNIT)
            out = out + dot(hidden[r], w)
        blocks.append(out)
    part(core_ref, blocks, keep_ref, send_ref)


def pre_grad_of(pre, hidden_grad):
    gate, up = pre[:, :UNIT], pre[:, UNIT:]
    sigma = jax.nn.sigmoid(gate)
    gate_grad = hidden_grad * up * sigma * (1.0 + gate * (1.0 - sigma))
    up_grad = hidden_grad * gate * sigma
    return jnp.concatenate([gate_grad, up_grad], 1).astype(BF16)


def backward_body(core_ref, grads_ref, pre_ref, w0, w1, w2a, w2b, w3, keep_ref, send_ref):
    blocks = []
    packed = packed_refs((w0, w1, w2a, w2b, w3))
    pre_grads = []
    for r in range(Y):
        hidden_grad = jnp.zeros((SLOTS, UNIT), F32)
        for b in range(Y):
            start = WIDTH + b * UNIT
            [(_, w)] = rows_of(packed[r], start, start + UNIT)
            piece = grads_ref[b // 2, :, (b % 2) * BLOCK : (b % 2 + 1) * BLOCK]
            hidden_grad = hidden_grad + dot(piece, w, CONTRACT_LAST)
        pre_grads.append(pre_grad_of(pre_ref[r], hidden_grad))
    for start in range(0, WIDTH, BLOCK):
        out = jnp.zeros((SLOTS, BLOCK), F32)
        for r in range(Y):
            [(_, w)] = rows_of(packed[r], start, start + BLOCK)
            out = out + dot(pre_grads[r], w, CONTRACT_LAST)
        blocks.append(out)
    part(core_ref, blocks, keep_ref, send_ref)


def block_of(ref, b):
    return ref[b // 2, :, (b % 2) * BLOCK : (b % 2 + 1) * BLOCK]


def again_body(core_ref, own_ref, near_ref, far_ref, w_own, w_other, pre_ref, hidden_ref, first_ref):
    first_ref[...] = jnp.where(core_ref[0] == 0, own_ref[...], far_ref[...])
    for g, rows_ref in enumerate((first_ref, near_ref)):
        for k, w in enumerate((w_own, w_other)):
            pre = dot(rows_ref[0], w[:HALF, :]) + dot(rows_ref[1], w[HALF:WIDTH, :])
            pre_ref[g, k] = pre
            gate, up = pre[:, :UNIT], pre[:, UNIT:]
            hidden_ref[g, k] = (gate * jax.nn.sigmoid(gate) * up).astype(BF16)


def weight_grads_body(
    core_ref, own_ref, near_ref, far_ref, rows0_ref, rows1_ref, pre_ref, hidden_ref, w_own, w_other,
    mine_ref, theirs_ref, first_ref,
):
    first_ref[...] = jnp.where(core_ref[0] == 0, own_ref[...], far_ref[...])
    grads, rows = (first_ref, near_ref), (rows0_ref, rows1_ref)
    for k, (w, out_ref) in enumerate(((w_own, mine_ref), (w_other, theirs_ref))):
        pre_grads = []
        for g in range(2):
            hidden_grad = jnp.zeros((SLOTS, UNIT), F32)
            for b in range(Y):
                down = w[WIDTH + b * UNIT : WIDTH + (b + 1) * UNIT, :]
                hidden_grad = hidden_grad + dot(block_of(grads[g], b), down, CONTRACT_LAST)
            pre_grads.append(pre_grad_of(pre_ref[g, k], hidden_grad))
        for b in range(Y):
            out_ref[b * BLOCK : (b + 1) * BLOCK, :] = sum(
                dot(block_of(rows[g], b), pre_grads[g], CONTRACT_FIRST) for g in range(2)
            ).astype(out_ref.dtype)
            out_ref[WIDTH + b * UNIT : WIDTH + (b + 1) * UNIT, :] = sum(
                dot(hidden_ref[g, k], block_of(grads[g], b), CONTRACT_FIRST) for g in range(2)
            ).astype(out_ref.dtype)


def loss_body(parts_ref, targets_away, scales_ref, gated_away, out_ref, targets_ref, gated_ref, sems):
    loads = [
        pltpu.make_async_copy(targets_away, targets_ref, sems.at[0]),
        pltpu.make_async_copy(gated_away, gated_ref, sems.at[1]),
    ]
    for load in loads:
        load.start()
    layer_out = parts_ref[0].astype(F32)
    for y in range(1, Y):
        layer_out = layer_out + parts_ref[y].astype(F32)
    for load in loads:
        load.wait()
    loss_grad = (scales_ref[...] * (layer_out - targets_ref[...].astype(F32))).astype(BF16)
    out_ref[...] = dot(gated_ref[...], loss_grad).astype(BF16)


def finish_body(own_ref, other_ref, gate_ref, up_ref, down_ref):
    for start in range(0, PACKED, BLOCK):
        rows = slice(start, start + BLOCK)
        value = own_ref[rows, :] + other_ref[rows, :].astype(F32)
        if start < WIDTH:
            gate_ref[rows, :] = value[:, :UNIT]
            up_ref[rows, :] = value[:, UNIT:]
        else:
            b = (start - WIDTH) // UNIT
            down_ref[:, b * BLOCK : (b + 1) * BLOCK] = value[:UNIT]
            down_ref[:, (b + 1) * BLOCK : (b + 2) * BLOCK] = value[UNIT:]


def shards(tokens, routes, route_gates, domains, domain_weight, targets, w_gate, w_up, w_down):
    count, width = tokens.shape
    chip, core = lax.axis_index("y"), lax.axis_index("c")

    own = pack(w_gate[0], w_up[0], w_down[0])
    one, three = shift(own, 1), shift(own, -1)
    weights = (own, one, shift(one[:CUT], 1), shift(three[CUT:], -1), three)

    select, gated = tables(routes, route_gates, chip * PLACES)
    my_tokens = lax.dynamic_slice(tokens, (0, core * HALF), (count, HALF))
    my_targets = lax.dynamic_slice(targets, (0, core * HALF), (count, HALF))
    picks = domains[:, None] == jnp.arange(domain_weight.shape[0], dtype=jnp.int32)[None, :]
    scales = jnp.sum(jnp.where(picks, domain_weight[None, :], 0.0), 1)

    core_id = core.reshape(1).astype(jnp.int32)
    half, halves, quarters = (SLOTS, HALF), (C, SLOTS, HALF), (Y, SLOTS, BLOCK)
    slot_rows = spread(over_experts(dot(select, my_tokens).astype(BF16)), "c", C)
    keep, send, pre = call(forward_body, [(half, BF16), (half, BF16), (quarters, F32)], core_id, slot_rows, *weights)
    returned = over_experts((keep.astype(F32) + swap(send).astype(F32)).astype(BF16))

    others, near_rows, far_rows = swap(own), near(slot_rows), far(slot_rows)
    quarter_out = dot(gated, returned, CONTRACT_FIRST).astype(BF16)
    parts = spread(quarter_out, "y", Y)
    parts, others, near_rows, far_rows = lax.optimization_barrier((parts, others, near_rows, far_rows))
    scratch = [pltpu.VMEM((count, HALF), BF16), pltpu.VMEM((SLOTS, count), BF16), pltpu.SemaphoreType.DMA((2,))]
    [sent] = call(
        loss_body, [(half, BF16)], parts, my_targets, scales[:, None], gated, scratch=scratch, away=(1, 3)
    )
    slot_grads = spread(over_experts(sent), "c", C)
    keep, send = call(backward_body, [(half, BF16), (half, BF16)], core_id, slot_grads, pre, *weights)
    row_sums = (keep.astype(F32) + swap(send).astype(F32)).astype(BF16)
    row_sums, late_grads, late_rows = lax.optimization_barrier((row_sums, slot_grads, slot_rows))
    grad_returned = over_experts(row_sums)

    outs = [((2, 2, SLOTS, BLOCK), F32), ((2, 2, SLOTS, UNIT), BF16), (halves, BF16)]
    pre_again, hidden_again, first_rows = call(
        again_body, outs, core_id, late_rows, near_rows, far_rows, own, others
    )
    mine, theirs = call(
        weight_grads_body, [((PACKED, BLOCK), F32), ((PACKED, BLOCK), BF16)],
        core_id, slot_grads, near(late_grads), far(late_grads), first_rows, near_rows, pre_again, hidden_again, own, others,
        scratch=[pltpu.VMEM(halves, BF16)],
    )
    outs = [((WIDTH, UNIT), F32), ((WIDTH, UNIT), F32), ((UNIT, WIDTH), F32)]
    grad_gate, grad_up, grad_down = call(finish_body, outs, mine, swap(theirs))

    quarter_input = dot(select, grad_returned, CONTRACT_FIRST).astype(BF16)
    my_grad = total(spread(quarter_input, "y", Y)).astype(BF16)
    other = swap(my_grad)
    grad_tokens = jnp.where(core == 0, jnp.concatenate([my_grad, other], 1), jnp.concatenate([other, my_grad], 1))
    return (grad_tokens, grad_gate[None], grad_up[None], grad_down[None])


def solution(mesh):
    fine = Mesh(mesh.devices.reshape(Y, C, X, Z), ("y", "c", "x", "z"))
    expert, dp = ("x", "z"), ("y", "c")
    return jax.shard_map(
        shards,
        mesh=fine,
        in_specs=(
            P(expert, None),
            P(expert, None),
            P(expert, None),
            P(expert),
            P(),
            P(expert, None),
            P(expert, None, dp),
            P(expert, None, dp),
            P(expert, dp, None),
        ),
        out_specs=(
            P(expert, None),
            P(expert, None, dp),
            P(expert, None, dp),
            P(expert, dp, None),
        ),
        check_vma=False,
    )
```
